32 devices in a mesh: rep: 8 (over z, core), fsdp: 4 (over y, x).
Axes of the slice: x: 2, y: 2, z: 4, core: 2. Of those that a mesh axis runs over, the one named last changes fastest.
Arguments:
- block_in: bfloat16 [8, 512, 1152], P('rep', 'fsdp'), may hold values from -6 to 6
- seq_lengths: int32 [8, 4], P('rep'), may hold values from 1 to 320, 512 in all within a row
- input_gain: bfloat16 [1152], P('fsdp'), may hold values from 0.5 to 1.5
- w_query: bfloat16 [1152, 1024], P('fsdp'), may hold values from -0.1875 to 0.1875
- w_key: bfloat16 [1152, 256], P('fsdp'), may hold values from -0.1875 to 0.1875
- w_value: bfloat16 [1152, 256], P('fsdp'), may hold values from -0.1875 to 0.1875
- query_gain: bfloat16 [256], P('fsdp'), may hold values from 0.6 to 1.8
- key_gain: bfloat16 [256], P('fsdp'), may hold values from 0.6 to 1.8
- w_out: bfloat16 [1024, 1152], P('fsdp'), may hold values from -0.1875 to 0.1875
- post_attn_gain: bfloat16 [1152], P('fsdp'), may hold values from 0.5 to 1.5
- pre_ff_gain: bfloat16 [1152], P('fsdp'), may hold values from 0.5 to 1.5
- w_gate: bfloat16 [1152, 6912], P('fsdp'), may hold values from -0.1875 to 0.1875
- w_up: bfloat16 [1152, 6912], P('fsdp'), may hold values from -0.1875 to 0.1875
- w_down: bfloat16 [6912, 1152], P('fsdp'), may hold values from -0.078125 to 0.078125
- post_ff_gain: bfloat16 [1152], P('fsdp'), may hold values from 0.5 to 1.5
- cotangent: bfloat16 [8, 512, 1152], P('rep', 'fsdp'), may hold values from -6 to 6
Outputs:
- block_out: bfloat16 [8, 512, 1152], P('rep', 'fsdp')
- grad_input: bfloat16 [8, 512, 1152], P('rep', 'fsdp')
- grad_input_gain: float32 [1152], P('fsdp')
- grad_w_query: float32 [1152, 1024], P('fsdp')
- grad_w_key: float32 [1152, 256], P('fsdp')
- grad_w_value: float32 [1152, 256], P('fsdp')
- grad_query_gain: float32 [256], P('fsdp')
- grad_key_gain: float32 [256], P('fsdp')
- grad_w_out: float32 [1024, 1152], P('fsdp')
- grad_post_attn_gain: float32 [1152], P('fsdp')
- grad_pre_ff_gain: float32 [1152], P('fsdp')
- grad_w_gate: float32 [1152, 6912], P('fsdp')
- grad_w_up: float32 [1152, 6912], P('fsdp')
- grad_w_down: float32 [6912, 1152], P('fsdp')
- grad_post_ff_gain: float32 [1152], P('fsdp')
The draws below stay inside these ranges and needn't reach their ends.
Inputs may be any that keep to these rules, and one draw needn't show every extreme that they name: `seq_lengths`: each group's 4 lengths sum to 512, and the longest of them is exactly 320 in every group.
All inputs are finite; a program needn't handle non-finite values.
Results may differ from the reference program's by a relative error of at most 0.017.
Values may be sent and summed in bfloat16 or wider, within the bound.
No kernel may reach another device: no remote copies, remote signals or barrier semaphores. Data moves between devices by JAX's collectives and lax.ppermute only.
A program may use at most 256 MiB of HBM per device.

```python
import math
import jax
import jax.numpy as jnp
import numpy as np
from jax import lax

D = 1152
HEADS = 4
HD = 256
FF = 6912
WINDOW = 512
SEQS = 4
GROUP_TOK = 512
MAXLEN = 320
N_REP = 8


def draw_query_gain(key, part):
    own_key = jax.random.fold_in(key, 101)
    return jax.random.uniform(own_key, (HD,), jnp.float32, 0.6, 1.6).astype(jnp.bfloat16)


def draw_key_gain(key, part):
    own_key = jax.random.fold_in(key, 211)
    return jax.random.uniform(own_key, (HD,), jnp.float32, 0.6, 1.6).astype(jnp.bfloat16)


def steps_of(key, shape, split, smallest, top_value):
    level, own = 1.0, jax.random.fold_in(key, 6)
    for position, shards_of in split:
        steps = jnp.exp(jax.random.uniform(jax.random.fold_in(own, position), (shards_of,), jnp.float32, smallest / len(split), top_value / len(split)))
        level = level * jnp.repeat(steps, shape[position] // shards_of).reshape([-1 if axis == position else 1 for axis in range(len(shape))])
    return level


def profile(amount, total, reach, skew):
    loads = [(1 << 20) // math.isqrt(standing ** skew) + 1 for standing in range(2, amount + 1)]
    spare, counts = total - reach - (amount - 1), [1] * (amount - 1)
    while spare > 0:
        free = [i for i in range(amount - 1) if counts[i] < reach]
        whole, remaining = sum([loads[i] for i in free]), spare
        for i in free:
            addition = min(reach - counts[i], max(1, remaining * loads[i] // whole), spare)
            counts[i] = counts[i] + addition
            spare = spare - addition
    return np.array([reach] + counts)


def uneven(stream_key, number_of, total, limit, skew):
    if number_of == 2:
        one = jax.random.randint(stream_key, (), max(1, total - limit), min(limit, total - 1) + 1)
        return jnp.stack([one, total - one])
    sizes = jnp.asarray(profile(number_of, total, limit, skew), jnp.int32)
    pairs = (number_of - 1) // 2
    donor, sink = sizes[1:1 + 2 * pairs:2], sizes[2:2 + 2 * pairs:2]
    slack = jnp.minimum(donor - 1, limit - sink)
    passed = jax.random.randint(jax.random.fold_in(stream_key, 1), (pairs,), 0, 1 << 20) % (slack + 1)
    sizes = sizes.at[1:1 + 2 * pairs:2].set(donor - passed).at[2:2 + 2 * pairs:2].set(sink + passed)
    return sizes[jax.random.permutation(jax.random.fold_in(stream_key, 2), number_of)]


def gaussian(key, shape, deviation, most, pieces=(), kind=jnp.bfloat16):
    drawn = jax.random.normal(key, shape, jnp.float32) * deviation
    if len(pieces) > 0:
        drawn = steps_of(key, shape, pieces, -0.22, 0.18) * drawn
    return jnp.clip(drawn, min=-most, max=most).astype(kind)


def setup_inputs(seed: int = 0) -> dict:
    arg_keys = jax.random.split(jax.random.key(seed), 17)
    block_in = gaussian(arg_keys[0], (N_REP, GROUP_TOK, D), 1.0, 6.0, ((0, 8), (1, 4)))
    seq_lengths = jax.vmap(lambda own: uneven(own, SEQS, GROUP_TOK, MAXLEN, 2))(jax.random.split(arg_keys[1], N_REP)).reshape((N_REP, SEQS)).astype(jnp.int32)
    input_gain = jnp.clip(1.0 + 0.1 * jax.random.normal(arg_keys[2], (D,), jnp.float32), 0.5, 1.5).astype(jnp.bfloat16)
    w_query = gaussian(arg_keys[3], (D, HEADS * HD), D ** -0.5, 0.1875, ((0, 4),))
    w_key = gaussian(arg_keys[4], (D, HD), D ** -0.5, 0.1875, ((0, 4),))
    w_value = gaussian(arg_keys[5], (D, HD), D ** -0.5, 0.1875, ((0, 4),))
    query_gain = draw_query_gain(jax.random.fold_in(arg_keys[16], 71), 0)
    key_gain = draw_key_gain(jax.random.fold_in(arg_keys[16], 71), 0)
    w_out = gaussian(arg_keys[8], (HEADS * HD, D), (HEADS * HD) ** -0.5, 0.1875, ((0, 4),))
    post_attn_gain = jnp.clip(1.0 + 0.1 * jax.random.normal(arg_keys[9], (D,), jnp.float32), 0.5, 1.5).astype(jnp.bfloat16)
    pre_ff_gain = jnp.clip(1.0 + 0.1 * jax.random.normal(arg_keys[10], (D,), jnp.float32), 0.5, 1.5).astype(jnp.bfloat16)
    w_gate = gaussian(arg_keys[11], (D, FF), D ** -0.5, 0.1875, ((0, 4),))
    w_up = gaussian(arg_keys[12], (D, FF), D ** -0.5, 0.1875, ((0, 4),))
    w_down = gaussian(arg_keys[13], (FF, D), FF ** -0.5, 0.078125, ((0, 4),))
    post_ff_gain = jnp.clip(1.0 + 0.1 * jax.random.normal(arg_keys[14], (D,), jnp.float32), 0.5, 1.5).astype(jnp.bfloat16)
    cotangent = gaussian(arg_keys[15], (N_REP, GROUP_TOK, D), 1.0, 6.0, ((0, 8), (1, 4)))
    return {"block_in": block_in, "seq_lengths": seq_lengths, "input_gain": input_gain, "w_query": w_query, "w_key": w_key, "w_value": w_value, "query_gain": query_gain, "key_gain": key_gain, "w_out": w_out, "post_attn_gain": post_attn_gain, "pre_ff_gain": pre_ff_gain, "w_gate": w_gate, "w_up": w_up, "w_down": w_down, "post_ff_gain": post_ff_gain, "cotangent": cotangent}


EPSILON = 1e-06
NEG_FILL = -1e+30
GELU_SCALE = math.sqrt(2.0 / math.pi)

def rms_factor(values):
    return lax.rsqrt(lax.optimization_barrier(jnp.mean(values * values, axis=-1, keepdims=True)) + EPSILON)

def norm_back(grad_unit, unit_vals, factor):
    return factor * (grad_unit - unit_vals * lax.optimization_barrier(jnp.mean(grad_unit * unit_vals, axis=-1, keepdims=True)))

def gelu_parts(values):
    cubic = values * values * values
    tangent = jnp.tanh(GELU_SCALE * (values + 0.044715 * cubic))
    result = 0.5 * values * (1.0 + tangent)
    slope = 0.5 * (1.0 + tangent) + 0.5 * values * (1.0 - tangent * tangent) * GELU_SCALE * (1.0 + 3.0 * 0.044715 * values * values)
    return (result, slope)

def rope_tables(positions, head_width):
    half_width = head_width // 2
    freqs = 10000.0 ** (-2.0 * jnp.arange(half_width, dtype=jnp.float32) / head_width)
    angles = positions.astype(jnp.float32)[:, None] * freqs[None, :]
    return (jnp.cos(angles), jnp.sin(angles))

def rotate(values, cos_table, sin_table):
    half_width = values.shape[-1] // 2
    lower_half = values[..., :half_width]
    upper_half = values[..., half_width:]
    return jnp.concatenate([lower_half * cos_table - upper_half * sin_table, upper_half * cos_table + lower_half * sin_table], axis=-1)

def unrotate(grads, cos_table, sin_table):
    half_width = grads.shape[-1] // 2
    lower_half = grads[..., :half_width]
    upper_half = grads[..., half_width:]
    return jnp.concatenate([lower_half * cos_table + upper_half * sin_table, upper_half * cos_table - lower_half * sin_table], axis=-1)

def locate(row_ids, lengths):
    ends = jnp.cumsum(lengths).astype(jnp.int32)
    starts = ends - lengths
    segment = lax.optimization_barrier(jnp.sum((row_ids[:, None] >= ends[None, :]).astype(jnp.int32), axis=1))
    choose = segment[:, None] == jnp.arange(lengths.shape[0], dtype=jnp.int32)[None, :]
    first_row = lax.optimization_barrier(jnp.sum(jnp.where(choose, starts[None, :], 0), axis=1))
    return (segment, row_ids - first_row)

def window_mask(query_rows, query_seg, key_rows, key_seg):
    distance = query_rows[:, None] - key_rows[None, :]
    return (query_seg[:, None] == key_seg[None, :]) & (distance >= 0) & (distance < WINDOW) & (key_rows[None, :] >= 0)

def fdot(first_op, second_op):
    return jnp.dot(first_op, second_op, preferred_element_type=jnp.float32)

def masked_scores(query_rot, key_rot, allowed, score_scale):
    scores = jnp.einsum('qhd,kd->hqk', query_rot.astype(jnp.float32), key_rot.astype(jnp.float32)) * score_scale
    return jnp.where(allowed[None], scores, NEG_FILL)

def one_group(weights, block_in, lengths, cotangent):
    input_gain, w_query, w_key, w_value, query_gain, key_gain, w_out, post_attn_gain, pre_ff_gain, w_gate, w_up, w_down, post_ff_gain = weights
    total_rows = block_in.shape[0]
    row_ids = jnp.arange(total_rows, dtype=jnp.int32)
    segment, positions = locate(row_ids, lengths)
    allowed = window_mask(row_ids, segment, row_ids, segment)
    cos_table, sin_table = rope_tables(positions, HD)
    score_scale = HD ** (-0.5)
    gain_in = input_gain.astype(jnp.float32)
    gain_q = query_gain.astype(jnp.float32)
    gain_k = key_gain.astype(jnp.float32)
    gain_pa = post_attn_gain.astype(jnp.float32)
    gain_pf = pre_ff_gain.astype(jnp.float32)
    gain_pff = post_ff_gain.astype(jnp.float32)
    resid_in = block_in.astype(jnp.float32)
    factor_in = rms_factor(resid_in)
    unit_in = resid_in * factor_in
    normed_in = (unit_in * gain_in).astype(jnp.bfloat16)
    query_raw = fdot(normed_in, w_query).reshape(total_rows, HEADS, HD)
    key_raw = fdot(normed_in, w_key)
    value_bf = fdot(normed_in, w_value).astype(jnp.bfloat16)
    factor_q = rms_factor(query_raw)
    unit_q = query_raw * factor_q
    factor_k = rms_factor(key_raw)
    unit_k = key_raw * factor_k
    query_rot = rotate(unit_q * gain_q, cos_table[:, None, :], sin_table[:, None, :]).astype(jnp.bfloat16)
    key_rot = rotate(unit_k * gain_k, cos_table, sin_table).astype(jnp.bfloat16)
    scores = masked_scores(query_rot, key_rot, allowed, score_scale)
    row_max = lax.optimization_barrier(jnp.max(scores, axis=-1, keepdims=True))
    log_total = row_max + jnp.log(lax.optimization_barrier(jnp.sum(jnp.exp(scores - row_max), axis=-1, keepdims=True)))
    probs_bf = jnp.exp(scores - log_total).astype(jnp.bfloat16)
    attended3 = jnp.einsum('hqk,kd->qhd', probs_bf.astype(jnp.float32), value_bf.astype(jnp.float32)).astype(jnp.bfloat16)
    attended = attended3.reshape(total_rows, HEADS * HD)
    attn_proj = fdot(attended, w_out)
    factor_pa = rms_factor(attn_proj)
    unit_pa = attn_proj * factor_pa
    hidden = resid_in + unit_pa * gain_pa
    factor_hid = rms_factor(hidden)
    unit_hid = hidden * factor_hid
    normed_ff = (unit_hid * gain_pf).astype(jnp.bfloat16)
    gate_proj = fdot(normed_ff, w_gate)
    up_proj = fdot(normed_ff, w_up)
    gelu_value, gelu_slope = gelu_parts(gate_proj)
    mixed = (gelu_value * up_proj).astype(jnp.bfloat16)
    ff_proj = fdot(mixed, w_down)
    factor_ff = rms_factor(ff_proj)
    unit_ff = ff_proj * factor_ff
    block_out = (hidden + unit_ff * gain_pff).astype(jnp.bfloat16)
    grad_out = cotangent.astype(jnp.float32)
    grad_gain_pff = lax.optimization_barrier(jnp.sum(grad_out * unit_ff, axis=0))
    grad_ff_proj = norm_back(grad_out * gain_pff, unit_ff, factor_ff).astype(jnp.bfloat16)
    grad_w_down = fdot(mixed.T, grad_ff_proj)
    grad_mixed = fdot(grad_ff_proj, w_down.T)
    grad_gate = (grad_mixed * up_proj * gelu_slope).astype(jnp.bfloat16)
    grad_up = (grad_mixed * gelu_value).astype(jnp.bfloat16)
    grad_w_gate = fdot(normed_ff.T, grad_gate)
    grad_w_up = fdot(normed_ff.T, grad_up)
    grad_normed_ff = fdot(grad_gate, w_gate.T) + fdot(grad_up, w_up.T)
    grad_gain_pf = lax.optimization_barrier(jnp.sum(grad_normed_ff * unit_hid, axis=0))
    grad_hidden = grad_out + norm_back(grad_normed_ff * gain_pf, unit_hid, factor_hid)
    grad_gain_pa = lax.optimization_barrier(jnp.sum(grad_hidden * unit_pa, axis=0))
    grad_attn_proj = norm_back(grad_hidden * gain_pa, unit_pa, factor_pa).astype(jnp.bfloat16)
    grad_w_out = fdot(attended.T, grad_attn_proj)
    grad_attended = fdot(grad_attn_proj, w_out.T).astype(jnp.bfloat16).reshape(total_rows, HEADS, HD)
    scores_again = masked_scores(query_rot, key_rot, allowed, score_scale)
    probs = jnp.exp(scores_again - log_total)
    probs_again = probs.astype(jnp.bfloat16)
    grad_probs = jnp.einsum('qhd,kd->hqk', grad_attended.astype(jnp.float32), value_bf.astype(jnp.float32))
    delta = lax.optimization_barrier(jnp.sum(grad_attended.astype(jnp.float32) * attended3.astype(jnp.float32), axis=-1)).T[:, :, None]
    grad_scores = (probs * (grad_probs - delta) * score_scale).astype(jnp.bfloat16)
    grad_value = jnp.einsum('hqk,qhd->kd', probs_again.astype(jnp.float32), grad_attended.astype(jnp.float32)).astype(jnp.bfloat16)
    grad_query_rot = jnp.einsum('hqk,kd->qhd', grad_scores.astype(jnp.float32), key_rot.astype(jnp.float32))
    grad_key_rot = jnp.einsum('hqk,qhd->kd', grad_scores.astype(jnp.float32), query_rot.astype(jnp.float32))
    grad_unit_q = unrotate(grad_query_rot, cos_table[:, None, :], sin_table[:, None, :])
    grad_unit_k = unrotate(grad_key_rot, cos_table, sin_table)
    grad_gain_q = lax.optimization_barrier(jnp.sum(grad_unit_q * unit_q, axis=(0, 1)))
    grad_gain_k = lax.optimization_barrier(jnp.sum(grad_unit_k * unit_k, axis=0))
    grad_query = norm_back(grad_unit_q * gain_q, unit_q, factor_q).astype(jnp.bfloat16).reshape(total_rows, HEADS * HD)
    grad_key = norm_back(grad_unit_k * gain_k, unit_k, factor_k).astype(jnp.bfloat16)
    grad_w_query = fdot(normed_in.T, grad_query)
    grad_w_key = fdot(normed_in.T, grad_key)
    grad_w_value = fdot(normed_in.T, grad_value)
    grad_normed_in = fdot(grad_query, w_query.T) + fdot(grad_key, w_key.T) + fdot(grad_value, w_value.T)
    grad_gain_in = lax.optimization_barrier(jnp.sum(grad_normed_in * unit_in, axis=0))
    grad_input = (grad_hidden + norm_back(grad_normed_in * gain_in, unit_in, factor_in)).astype(jnp.bfloat16)
    grads = (grad_gain_in, grad_w_query, grad_w_key, grad_w_value, grad_gain_q, grad_gain_k, grad_w_out, grad_gain_pa, grad_gain_pf, grad_w_gate, grad_w_up, grad_w_down, grad_gain_pff)
    return (block_out, grad_input, grads)

def reference(block_in, seq_lengths, input_gain, w_query, w_key, w_value, query_gain, key_gain, w_out, post_attn_gain, pre_ff_gain, w_gate, w_up, w_down, post_ff_gain, cotangent):
    weights = (input_gain, w_query, w_key, w_value, query_gain, key_gain, w_out, post_attn_gain, pre_ff_gain, w_gate, w_up, w_down, post_ff_gain)
    initial = tuple((jnp.zeros(weight.shape, jnp.float32) for weight in weights))

    def step_group(totals, inputs):
        group_in, group_lengths, group_cot = inputs
        group_out, group_grad, grads = one_group(weights, group_in, group_lengths, group_cot)
        totals = tuple((total + grad for total, grad in zip(totals, grads)))
        return (totals, (group_out, group_grad))
    totals, (block_out, grad_input) = lax.scan(step_group, initial, (block_in, seq_lengths, cotangent))
    return (block_out, grad_input) + totals
```

```python
import math

import jax
import jax.numpy as jnp
from jax import lax
from jax.sharding import PartitionSpec as P

WINDOW = 512


EPSILON = 1e-06
NEG_FILL = -1e30
GELU_SCALE = math.sqrt(2.0 / math.pi)


def swap_cores(block):
    return lax.ppermute(block, "rep", [(i, i ^ 1) for i in range(lax.axis_size("rep"))])


def to_peer(block, step):
    return lax.ppermute(block, "fsdp", [(i, i ^ step) for i in range(lax.axis_size("fsdp"))])


def place(buffer, block, index):
    return lax.dynamic_update_index_in_dim(buffer, block, index, 0)


def pick(blocks, index):
    return lax.dynamic_index_in_dim(blocks, index, 0, keepdims=False)


def gather_blocks(block):
    own = lax.axis_index("fsdp")
    peers = lax.axis_size("fsdp")
    received = [block] + [to_peer(block, step) for step in range(1, peers)]
    buffer = jnp.zeros((peers,) + block.shape, block.dtype)
    for step in range(peers):
        buffer = place(buffer, received[step], own ^ step)
    return buffer


def exchange_blocks(block_for):
    own = lax.axis_index("fsdp")
    peers = lax.axis_size("fsdp")
    return [block_for(own)] + [to_peer(block_for(own ^ step), step) for step in range(1, peers)]


def in_order(received):
    own = lax.axis_index("fsdp")
    buffer = jnp.zeros((len(received),) + received[0].shape, received[0].dtype)
    for step, block in enumerate(received):
        buffer = place(buffer, block, own ^ step)
    return buffer


def join_halves(mine, core, axis):
    other = swap_cores(mine)
    first = core == 0
    return jnp.stack([jnp.where(first, mine, other), jnp.where(first, other, mine)], axis)


def sum_to_owner(partial):
    own = lax.axis_index("fsdp")
    peers = lax.axis_size("fsdp")
    blocks = partial.reshape((peers, partial.shape[0] // peers) + partial.shape[1:])
    total = pick(blocks, own)
    for step in range(1, peers):
        sent = pick(blocks, own ^ step).astype(jnp.bfloat16)
        total = total + to_peer(sent, step).astype(jnp.float32)
    return total


def sum_over_cores(halves, core):
    mine = pick(halves, core)
    other = swap_cores(pick(halves, 1 - core).astype(jnp.bfloat16))
    return (mine + other.astype(jnp.float32)).astype(jnp.bfloat16)


def add_rounded(first_op, second_op):
    return (first_op.astype(jnp.float32) + second_op.astype(jnp.float32)).astype(jnp.bfloat16)


def along_line(block, moves):
    pairs = [(2 * i + core, 2 * j + core) for i, j in moves for core in (0, 1)]
    return lax.ppermute(block, "rep", pairs)


def sum_over_pairs(block):
    pairs = lax.axis_size("rep") // 2
    if pairs != 4:
        step = 1
        while step < pairs:
            block = add_rounded(block, along_line(block, [(i, i ^ step) for i in range(pairs)]))
            step = 2 * step
        return block
    pair = lax.axis_index("rep") // 2
    inner = (pair == 1) | (pair == 2)
    block = add_rounded(block, along_line(block, [(0, 1), (3, 2)]))
    block = add_rounded(block, along_line(block, [(1, 2), (2, 1)]))
    return jnp.where(inner, block, along_line(block, [(1, 0), (2, 3)]))


def rms_factor(values):
    return lax.rsqrt(jnp.mean(values * values, axis=-1, keepdims=True) + EPSILON)


def norm_back(grad_unit, unit_vals, factor):
    return factor * (
        grad_unit - unit_vals * jnp.mean(grad_unit * unit_vals, axis=-1, keepdims=True)
    )


def gelu_parts(values):
    cubic = values * values * values
    tangent = jnp.tanh(GELU_SCALE * (values + 0.044715 * cubic))
    result = 0.5 * values * (1.0 + tangent)
    slope = 0.5 * (1.0 + tangent) + 0.5 * values * (1.0 - tangent * tangent) * GELU_SCALE * (
        1.0 + 3.0 * 0.044715 * values * values
    )
    return (result, slope)


def rope_tables(positions, head_width):
    half_width = head_width // 2
    freqs = 10000.0 ** (-2.0 * jnp.arange(half_width, dtype=jnp.float32) / head_width)
    angles = positions.astype(jnp.float32)[:, None] * freqs[None, :]
    return (jnp.cos(angles), jnp.sin(angles))


def rotate(values, cos_table, sin_table):
    half_width = values.shape[-1] // 2
    lower_half = values[..., :half_width]
    upper_half = values[..., half_width:]
    return jnp.concatenate(
        [
            lower_half * cos_table - upper_half * sin_table,
            upper_half * cos_table + lower_half * sin_table,
        ],
        axis=-1,
    )


def unrotate(grads, cos_table, sin_table):
    half_width = grads.shape[-1] // 2
    lower_half = grads[..., :half_width]
    upper_half = grads[..., half_width:]
    return jnp.concatenate(
        [
            lower_half * cos_table + upper_half * sin_table,
            upper_half * cos_table - lower_half * sin_table,
        ],
        axis=-1,
    )


def locate(row_ids, lengths):
    ends = jnp.cumsum(lengths)
    starts = ends - lengths
    segment = jnp.sum((row_ids[:, None] >= ends[None, :]).astype(jnp.int32), axis=1)
    choose = segment[:, None] == jnp.arange(lengths.shape[0], dtype=jnp.int32)[None, :]
    first_row = jnp.sum(jnp.where(choose, starts[None, :], 0), axis=1)
    return (segment, row_ids - first_row)


def window_mask(query_rows, query_seg, key_rows, key_seg):
    distance = query_rows[:, None] - key_rows[None, :]
    return (
        (query_seg[:, None] == key_seg[None, :])
        & (distance >= 0)
        & (distance < WINDOW)
        & (key_rows[None, :] >= 0)
    )


def fdot(first_op, second_op):
    return jnp.dot(first_op, second_op, preferred_element_type=jnp.float32)


def times_transposed(first_op, second_op):
    return lax.dot_general(
        first_op, second_op, (((1,), (1,)), ((), ())), preferred_element_type=jnp.float32
    )


def outer_sum(first_op, second_op):
    return lax.dot_general(
        first_op, second_op, (((0,), (0,)), ((), ())), preferred_element_type=jnp.float32
    )


def body(
    block_in,
    seq_lengths,
    input_gain,
    w_query,
    w_key,
    w_value,
    query_gain,
    key_gain,
    w_out,
    post_attn_gain,
    pre_ff_gain,
    w_gate,
    w_up,
    w_down,
    post_ff_gain,
    cotangent,
):
    bf16 = jnp.bfloat16
    f32 = jnp.float32
    own = lax.axis_index("fsdp")
    peers = lax.axis_size("fsdp")
    core = lax.axis_index("rep") % 2
    rows_here, width = block_in.shape[1:]
    rows = rows_here * peers
    head_width = w_key.shape[1]
    num_heads = w_query.shape[1] // head_width
    parts = peers // num_heads
    query_count = rows // parts
    head = own // parts
    query_start = (own % parts) * query_count
    slice_rows = w_gate.shape[0]
    half_rows = slice_rows // 2
    columns = w_down.shape[0]
    out_rows = w_out.shape[0]
    gain_slice = query_gain.shape[0]

    gain_parts = (input_gain, post_attn_gain, pre_ff_gain, post_ff_gain, query_gain, key_gain)
    gain_line = jnp.concatenate(gain_parts)
    gain_block = jnp.pad(gain_line, (0, 16 * width - gain_line.shape[0])).reshape(16, width)
    packed = gather_blocks(jnp.concatenate([block_in[0], gain_block]))
    resid_in = packed[:, :rows_here].reshape(rows, width).astype(f32)
    gain_lines = packed[:, rows_here : rows_here + 2].reshape(peers, 2 * width).astype(f32)
    gains = []
    start = 0
    for part in gain_parts:
        gains.append(gain_lines[:, start : start + part.shape[0]].reshape(-1))
        start = start + part.shape[0]
    gain_in, gain_pa, gain_pf, gain_pff, gain_q, gain_k = gains

    half_of = lambda matrix: pick(matrix.reshape(2, matrix.shape[0] // 2, matrix.shape[1]), core)
    query_half = half_of(w_query)
    kv_half = jnp.concatenate([half_of(w_key), half_of(w_value)], axis=1)

    def attn_block(peer):
        mine = lax.dynamic_slice_in_dim(query_half, (peer // parts) * head_width, head_width, 1)
        return jnp.concatenate([mine, kv_half], axis=1)

    qkv_w = join_halves(in_order(exchange_blocks(attn_block)), core, 1)
    qkv_w = qkv_w.reshape(width, 3 * head_width)
    out_w = join_halves(gather_blocks(half_of(w_out)), core, 1).reshape(-1, width)

    gate_half = half_of(w_gate)
    up_half = half_of(w_up)

    def ff_block(peer):
        first = lax.dynamic_slice_in_dim(gate_half, peer * columns, columns, 1)
        second = lax.dynamic_slice_in_dim(up_half, peer * columns, columns, 1)
        return jnp.stack([first, second])

    ff_w = join_halves(in_order(exchange_blocks(ff_block)), core, 2)
    gate_w = ff_w[:, 0].reshape(width, columns)
    up_w = ff_w[:, 1].reshape(width, columns)

    row_ids = jnp.arange(rows, dtype=jnp.int32)
    segment, positions = locate(row_ids, seq_lengths[0])
    cos_table, sin_table = rope_tables(positions, head_width)
    own_queries = lambda array: (
        array if parts == 1 else lax.dynamic_slice_in_dim(array, query_start, query_count, 0)
    )
    query_ids = own_queries(row_ids)
    query_seg = own_queries(segment)
    query_cos = own_queries(cos_table)
    query_sin = own_queries(sin_table)
    allowed = window_mask(query_ids, query_seg, row_ids, segment)
    score_scale = head_width ** (-0.5)
    unit_in = resid_in * rms_factor(resid_in)
    normed_in = (unit_in * gain_in).astype(bf16)
    qkv = fdot(normed_in, qkv_w)
    query_raw = own_queries(qkv[:, :head_width])
    key_raw = qkv[:, head_width : 2 * head_width]
    value_bf = qkv[:, 2 * head_width :].astype(bf16)
    factor_q = rms_factor(query_raw)
    unit_q = query_raw * factor_q
    factor_k = rms_factor(key_raw)
    unit_k = key_raw * factor_k
    query_rot = rotate(unit_q * gain_q, query_cos, query_sin).astype(bf16)
    key_rot = rotate(unit_k * gain_k, cos_table, sin_table).astype(bf16)
    scores = jnp.where(allowed, times_transposed(query_rot, key_rot) * score_scale, NEG_FILL)
    row_max = jnp.max(scores, axis=-1, keepdims=True)
    log_total = row_max + jnp.log(jnp.sum(jnp.exp(scores - row_max), axis=-1, keepdims=True))
    probs = jnp.exp(scores - log_total)
    probs_bf = probs.astype(bf16)
    attended_own = fdot(probs_bf, value_bf).astype(bf16)
    attended_heads = gather_blocks(attended_own).reshape(num_heads, rows, head_width)
    attended = jnp.concatenate([attended_heads[i] for i in range(num_heads)], axis=1)
    attn_proj = fdot(attended, out_w)
    factor_pa = rms_factor(attn_proj)
    unit_pa = attn_proj * factor_pa
    hidden = resid_in + unit_pa * gain_pa
    factor_hid = rms_factor(hidden)
    unit_hid = hidden * factor_hid
    normed_ff = (unit_hid * gain_pf).astype(bf16)

    gate_proj = fdot(normed_ff, gate_w)
    up_proj = fdot(normed_ff, up_w)
    gelu_value, gelu_slope = gelu_parts(gate_proj)
    mixed = (gelu_value * up_proj).astype(bf16)
    ff_proj = sum_to_owner(fdot(mixed, w_down))
    own_rows = lambda array: lax.dynamic_slice_in_dim(array, own * rows_here, rows_here, 0)
    hidden_own = own_rows(hidden)
    factor_ff = rms_factor(ff_proj)
    unit_ff = ff_proj * factor_ff
    block_out = (hidden_own + unit_ff * gain_pff).astype(bf16)
    grad_out = cotangent[0].astype(f32)
    grad_gain_pff = jnp.sum(grad_out * unit_ff, axis=0)
    grad_ff_own = norm_back(grad_out * gain_pff, unit_ff, factor_ff).astype(bf16)
    grad_ff_proj = gather_blocks(grad_ff_own).reshape(rows, width)
    grad_mixed = times_transposed(grad_ff_proj, w_down)
    grad_gate = (grad_mixed * up_proj * gelu_slope).astype(bf16)
    grad_up = (grad_mixed * gelu_value).astype(bf16)
    grad_normed_ff = sum_to_owner(
        times_transposed(grad_gate, gate_w) + times_transposed(grad_up, up_w)
    )
    factor_hid_own = own_rows(factor_hid)
    unit_hid_own = hidden_own * factor_hid_own
    grad_gain_pf = jnp.sum(grad_normed_ff * unit_hid_own, axis=0)
    grad_hidden = grad_out + norm_back(grad_normed_ff * gain_pf, unit_hid_own, factor_hid_own)
    factor_pa_own = own_rows(factor_pa)
    unit_pa_own = own_rows(attn_proj) * factor_pa_own
    grad_gain_pa = jnp.sum(grad_hidden * unit_pa_own, axis=0)
    grad_attn_own = norm_back(grad_hidden * gain_pa, unit_pa_own, factor_pa_own).astype(bf16)
    grad_attn_proj = gather_blocks(grad_attn_own).reshape(rows, width)

    down_grad = outer_sum(mixed, grad_ff_proj)
    gate_grad = outer_sum(normed_ff, grad_gate)
    up_grad = outer_sum(normed_ff, grad_up)
    chunks = 2

    def summed_chunks(halves):
        mine = sum_over_cores(halves, core)
        size = mine.shape[-2] // chunks
        return [sum_over_pairs(mine[..., i * size : (i + 1) * size, :]) for i in range(chunks)]

    down_chunks = summed_chunks(down_grad.reshape(2, columns // 2, width))
    share_down = jnp.concatenate([join_halves(part, core, 0) for part in down_chunks], axis=1)
    share_down = share_down.reshape(columns, width).astype(f32)

    def split_rows(grad):
        halves = grad.reshape(peers, 2, half_rows, columns).swapaxes(0, 1)
        pieces = []
        for part in summed_chunks(halves):
            received = in_order(exchange_blocks(lambda peer: pick(part, peer)))
            pieces.append(join_halves(received, core, 1))
        whole = jnp.concatenate(pieces, axis=2).reshape(peers, slice_rows, columns)
        return jnp.concatenate([whole[i] for i in range(peers)], axis=1).astype(f32)

    share_gate = split_rows(gate_grad)
    share_up = split_rows(up_grad)

    out_head = lax.dynamic_slice_in_dim(out_w, head * head_width, head_width, 0)
    attended_cols = lax.dynamic_slice_in_dim(attended, own * out_rows, out_rows, 1)
    if parts == 1:
        out_head = w_out
        attended_cols = attended_own
    out_grad = outer_sum(attended_cols, grad_attn_proj)
    grad_attended = times_transposed(own_queries(grad_attn_proj), out_head).astype(bf16)
    grad_probs = times_transposed(grad_attended, value_bf)
    delta = jnp.sum(
        grad_attended.astype(f32) * attended_own.astype(f32), axis=-1, keepdims=True
    )
    grad_scores = (probs * (grad_probs - delta) * score_scale).astype(bf16)
    grad_value = outer_sum(probs_bf, grad_attended).astype(bf16)
    grad_key_rot = outer_sum(grad_scores, query_rot)
    grad_query_rot = fdot(grad_scores, key_rot)
    grad_unit_q = unrotate(grad_query_rot, query_cos, query_sin)
    grad_unit_k = unrotate(grad_key_rot, cos_table, sin_table)
    grad_gain_q = jnp.sum(grad_unit_q * unit_q, axis=0)
    grad_gain_k = jnp.sum(grad_unit_k * unit_k, axis=0)
    grad_query = norm_back(grad_unit_q * gain_q, unit_q, factor_q).astype(bf16)
    grad_key = norm_back(grad_unit_k * gain_k, unit_k, factor_k).astype(bf16)
    if parts > 1:
        grad_query = lax.dynamic_update_slice_in_dim(
            jnp.zeros((rows, head_width), bf16), grad_query, query_start, 0
        )
    grad_qkv = jnp.concatenate([grad_query, grad_key, grad_value], axis=1)
    grad_normed_in = sum_to_owner(times_transposed(grad_qkv, qkv_w))
    qkv_grad = outer_sum(normed_in, grad_qkv)
    resid_own = block_in[0].astype(f32)
    factor_in_own = rms_factor(resid_own)
    unit_in_own = resid_own * factor_in_own
    grad_gain_in = jnp.sum(grad_normed_in * unit_in_own, axis=0)
    grad_input = (
        grad_hidden + norm_back(grad_normed_in * gain_in, unit_in_own, factor_in_own)
    ).astype(bf16)

    gain_grads = (
        grad_gain_in,
        grad_gain_pa,
        grad_gain_pf,
        grad_gain_pff,
        grad_gain_q,
        grad_gain_k,
    )
    gain_sums = jnp.concatenate([part.reshape(peers, -1) for part in gain_grads], axis=1)
    gain_count = gain_sums.shape[1] // 2
    gain_sums = jnp.pad(
        gain_sums.reshape(peers, 2, 1, gain_count),
        ((0, 0), (0, 0), (0, 15), (0, 3 * head_width - gain_count)),
    )
    attn_grads = jnp.concatenate(
        [qkv_grad.reshape(peers, 2, half_rows, 3 * head_width), gain_sums], axis=2
    )
    attn_half = sum_over_cores(attn_grads.swapaxes(0, 1), core)
    received = in_order(exchange_blocks(lambda peer: pick(attn_half, peer))).astype(f32)
    heads_sum = received[:, :half_rows, :head_width].reshape(
        num_heads, parts, half_rows, head_width
    )
    heads_sum = jnp.sum(heads_sum, axis=1)
    query_part = jnp.concatenate([heads_sum[i] for i in range(num_heads)], axis=1)
    rest = jnp.sum(received, axis=0)
    kv_part = rest[:half_rows, head_width:]
    out_half = sum_over_cores(out_grad.reshape(2, out_rows // 2, width), core)
    qkv_half = jnp.concatenate([query_part, kv_part], axis=1).astype(bf16)
    gain_half = rest[half_rows:].astype(bf16)
    qkv_rows = qkv_half.size // width
    half_out = out_rows // 2
    gain_pad = jnp.pad(gain_half[0], (0, 16 * width - gain_half.shape[1])).reshape(16, width)
    small = sum_over_pairs(
        jnp.concatenate([qkv_half.reshape(qkv_rows, width), out_half, gain_pad], axis=0)
    )
    small = join_halves(small, core, 0).astype(f32)
    share_qkv = small[:, :qkv_rows].reshape(slice_rows, (num_heads + 2) * head_width)
    query_width = num_heads * head_width
    share_query = share_qkv[:, :query_width]
    share_key = share_qkv[:, query_width : query_width + head_width]
    share_value = share_qkv[:, query_width + head_width :]
    share_out = small[:, qkv_rows : qkv_rows + half_out].reshape(out_rows, width)
    gain_line = small[:, qkv_rows + half_out, :gain_count].reshape(-1)
    sections = [slice_rows, slice_rows, slice_rows, slice_rows, gain_slice, gain_slice]
    shares = []
    start = 0
    for size in sections:
        shares.append(gain_line[start : start + size])
        start = start + size
    share_in, share_pa, share_pf, share_pff, share_q, share_k = shares
    return (
        block_out[None],
        grad_input[None],
        share_in,
        share_query,
        share_key,
        share_value,
        share_q,
        share_k,
        share_out,
        share_pa,
        share_pf,
        share_gate,
        share_up,
        share_down,
        share_pff,
    )


def solution(mesh):
    placed = (
        P("rep", "fsdp", None),
        P("rep", None),
        P("fsdp"),
        P("fsdp", None),
        P("fsdp", None),
        P("fsdp", None),
        P("fsdp"),
        P("fsdp"),
        P("fsdp", None),
        P("fsdp"),
        P("fsdp"),
        P("fsdp", None),
        P("fsdp", None),
        P("fsdp", None),
        P("fsdp"),
        P("rep", "fsdp", None),
    )
    return jax.shard_map(
        body,
        mesh=mesh,
        in_specs=placed,
        out_specs=(
            P("rep", "fsdp", None),
            P("rep", "fsdp", None),
            P("fsdp"),
            P("fsdp", None),
            P("fsdp", None),
            P("fsdp", None),
            P("fsdp"),
            P("fsdp"),
            P("fsdp", None),
            P("fsdp"),
            P("fsdp"),
            P("fsdp", None),
            P("fsdp", None),
            P("fsdp", None),
            P("fsdp"),
        ),
        check_vma=False,
    )
```

```python
import math

import jax
import jax.numpy as jnp
from jax import lax
from jax.sharding import PartitionSpec as P

WINDOW = 512


EPSILON = 1e-06
NEG_FILL = -1e30
GELU_SCALE = math.sqrt(2.0 / math.pi)


def swap_cores(block):
    return lax.ppermute(block, "rep", [(i, i ^ 1) for i in range(lax.axis_size("rep"))])


def to_peer(block, step):
    return lax.ppermute(block, "fsdp", [(i, i ^ step) for i in range(lax.axis_size("fsdp"))])


def place(buffer, block, index):
    return lax.dynamic_update_index_in_dim(buffer, block, index, 0)


def pick(blocks, index):
    return lax.dynamic_index_in_dim(blocks, index, 0, keepdims=False)


def gather_blocks(block):
    own = lax.axis_index("fsdp")
    peers = lax.axis_size("fsdp")
    received = [block] + [to_peer(block, step) for step in range(1, peers)]
    buffer = jnp.zeros((peers,) + block.shape, block.dtype)
    for step in range(peers):
        buffer = place(buffer, received[step], own ^ step)
    return buffer


def exchange_blocks(block_for):
    own = lax.axis_index("fsdp")
    peers = lax.axis_size("fsdp")
    return [block_for(own)] + [to_peer(block_for(own ^ step), step) for step in range(1, peers)]


def in_order(received):
    own = lax.axis_index("fsdp")
    buffer = jnp.zeros((len(received),) + received[0].shape, received[0].dtype)
    for step, block in enumerate(received):
        buffer = place(buffer, block, own ^ step)
    return buffer


def join_halves(mine, core, axis):
    other = swap_cores(mine)
    first = core == 0
    return jnp.stack([jnp.where(first, mine, other), jnp.where(first, other, mine)], axis)


def sum_to_owner(partial):
    own = lax.axis_index("fsdp")
    peers = lax.axis_size("fsdp")
    blocks = partial.reshape((peers, partial.shape[0] // peers) + partial.shape[1:])
    total = pick(blocks, own)
    for step in range(1, peers):
        sent = pick(blocks, own ^ step).astype(jnp.bfloat16)
        total = total + to_peer(sent, step).astype(jnp.float32)
    return total


def sum_over_cores(halves, core):
    mine = pick(halves, core)
    other = swap_cores(pick(halves, 1 - core).astype(jnp.bfloat16))
    return (mine + other.astype(jnp.float32)).astype(jnp.bfloat16)


def add_rounded(first_op, second_op):
    return (first_op.astype(jnp.float32) + second_op.astype(jnp.float32)).astype(jnp.bfloat16)


def along_line(block, moves):
    pairs = [(2 * i + core, 2 * j + core) for i, j in moves for core in (0, 1)]
    return lax.ppermute(block, "rep", pairs)


def sum_over_pairs(block):
    pairs = lax.axis_size("rep") // 2
    if pairs != 4:
        step = 1
        while step < pairs:
            block = add_rounded(block, along_line(block, [(i, i ^ step) for i in range(pairs)]))
            step = 2 * step
        return block
    pair = lax.axis_index("rep") // 2
    inner = (pair == 1) | (pair == 2)
    block = add_rounded(block, along_line(block, [(0, 1), (3, 2)]))
    block = add_rounded(block, along_line(block, [(1, 2), (2, 1)]))
    return jnp.where(inner, block, along_line(block, [(1, 0), (2, 3)]))


def across_pairs(block):
    pairs = lax.axis_size("rep") // 2
    return [along_line(block, [(i, i ^ step) for i in range(pairs)]) for step in range(1, pairs)]


def other_groups(own_rows, rows_of):
    own = lax.axis_index("fsdp")
    if lax.axis_size("fsdp") != 4:
        far = gather_blocks(jnp.stack(across_pairs(own_rows)))
        return far.reshape(-1, own_rows.shape[-1])
    sent = jnp.stack([own_rows, rows_of(own ^ 3)])
    received = jnp.stack(across_pairs(sent), 1)
    near = [to_peer(received[0], step) for step in (1, 2)]
    return jnp.stack([received[0], received[1]] + near).reshape(-1, own_rows.shape[-1])


def rms_factor(values):
    return lax.rsqrt(jnp.mean(values * values, axis=-1, keepdims=True) + EPSILON)


def norm_back(grad_unit, unit_vals, factor):
    return factor * (
        grad_unit - unit_vals * jnp.mean(grad_unit * unit_vals, axis=-1, keepdims=True)
    )


def gelu_parts(values):
    cubic = values * values * values
    tangent = jnp.tanh(GELU_SCALE * (values + 0.044715 * cubic))
    result = 0.5 * values * (1.0 + tangent)
    slope = 0.5 * (1.0 + tangent) + 0.5 * values * (1.0 - tangent * tangent) * GELU_SCALE * (
        1.0 + 3.0 * 0.044715 * values * values
    )
    return (result, slope)


def rope_tables(positions, head_width):
    half_width = head_width // 2
    freqs = 10000.0 ** (-2.0 * jnp.arange(half_width, dtype=jnp.float32) / head_width)
    angles = positions.astype(jnp.float32)[:, None] * freqs[None, :]
    return (jnp.cos(angles), jnp.sin(angles))


def rotate(values, cos_table, sin_table):
    half_width = values.shape[-1] // 2
    lower_half = values[..., :half_width]
    upper_half = values[..., half_width:]
    return jnp.concatenate(
        [
            lower_half * cos_table - upper_half * sin_table,
            upper_half * cos_table + lower_half * sin_table,
        ],
        axis=-1,
    )


def unrotate(grads, cos_table, sin_table):
    half_width = grads.shape[-1] // 2
    lower_half = grads[..., :half_width]
    upper_half = grads[..., half_width:]
    return jnp.concatenate(
        [
            lower_half * cos_table + upper_half * sin_table,
            upper_half * cos_table - lower_half * sin_table,
        ],
        axis=-1,
    )


def locate(row_ids, lengths):
    ends = jnp.cumsum(lengths)
    starts = ends - lengths
    segment = jnp.sum((row_ids[:, None] >= ends[None, :]).astype(jnp.int32), axis=1)
    choose = segment[:, None] == jnp.arange(lengths.shape[0], dtype=jnp.int32)[None, :]
    first_row = jnp.sum(jnp.where(choose, starts[None, :], 0), axis=1)
    return (segment, row_ids - first_row)


def window_mask(query_rows, query_seg, key_rows, key_seg):
    distance = query_rows[:, None] - key_rows[None, :]
    return (
        (query_seg[:, None] == key_seg[None, :])
        & (distance >= 0)
        & (distance < WINDOW)
        & (key_rows[None, :] >= 0)
    )


def fdot(first_op, second_op):
    return jnp.dot(first_op, second_op, preferred_element_type=jnp.float32)


def times_transposed(first_op, second_op):
    return lax.dot_general(
        first_op, second_op, (((1,), (1,)), ((), ())), preferred_element_type=jnp.float32
    )


def outer_sum(first_op, second_op):
    return lax.dot_general(
        first_op, second_op, (((0,), (0,)), ((), ())), preferred_element_type=jnp.float32
    )


def body(
    block_in,
    seq_lengths,
    input_gain,
    w_query,
    w_key,
    w_value,
    query_gain,
    key_gain,
    w_out,
    post_attn_gain,
    pre_ff_gain,
    w_gate,
    w_up,
    w_down,
    post_ff_gain,
    cotangent,
):
    bf16 = jnp.bfloat16
    f32 = jnp.float32
    own = lax.axis_index("fsdp")
    peers = lax.axis_size("fsdp")
    core = lax.axis_index("rep") % 2
    rows_here, width = block_in.shape[1:]
    rows = rows_here * peers
    head_width = w_key.shape[1]
    num_heads = w_query.shape[1] // head_width
    parts = peers // num_heads
    query_count = rows // parts
    head = own // parts
    query_start = (own % parts) * query_count
    slice_rows = w_gate.shape[0]
    half_rows = slice_rows // 2
    columns = w_down.shape[0]
    out_rows = w_out.shape[0]
    gain_slice = query_gain.shape[0]

    gain_parts = (input_gain, post_attn_gain, pre_ff_gain, post_ff_gain, query_gain, key_gain)
    gain_line = jnp.concatenate(gain_parts)
    gain_block = jnp.pad(gain_line, (0, 16 * width - gain_line.shape[0])).reshape(16, width)
    packed = gather_blocks(jnp.concatenate([block_in[0], gain_block]))
    resid_in = packed[:, :rows_here].reshape(rows, width).astype(f32)
    gain_lines = packed[:, rows_here : rows_here + 2].reshape(peers, 2 * width).astype(f32)
    gains = []
    start = 0
    for part in gain_parts:
        gains.append(gain_lines[:, start : start + part.shape[0]].reshape(-1))
        start = start + part.shape[0]
    gain_in, gain_pa, gain_pf, gain_pff, gain_q, gain_k = gains

    half_of = lambda matrix: pick(matrix.reshape(2, matrix.shape[0] // 2, matrix.shape[1]), core)
    query_half = half_of(w_query)
    kv_half = jnp.concatenate([half_of(w_key), half_of(w_value)], axis=1)

    def attn_block(peer):
        mine = lax.dynamic_slice_in_dim(query_half, (peer // parts) * head_width, head_width, 1)
        return jnp.concatenate([mine, kv_half], axis=1)

    qkv_blocks = in_order(exchange_blocks(attn_block))
    qkv_blocks, out_half = lax.optimization_barrier((qkv_blocks, half_of(w_out)))
    qkv_w = join_halves(qkv_blocks, core, 1).reshape(width, 3 * head_width)
    out_blocks = gather_blocks(out_half)
    out_w = join_halves(out_blocks, core, 1).reshape(-1, width)

    qkv_blocks, gate_half, up_half = lax.optimization_barrier(
        (qkv_blocks, half_of(w_gate), half_of(w_up))
    )

    def ff_block(peer):
        first = lax.dynamic_slice_in_dim(gate_half, peer * columns, columns, 1)
        second = lax.dynamic_slice_in_dim(up_half, peer * columns, columns, 1)
        return jnp.stack([first, second])

    ff_w = join_halves(in_order(exchange_blocks(ff_block)), core, 2)
    gate_w = ff_w[:, 0].reshape(width, columns)
    up_w = ff_w[:, 1].reshape(width, columns)

    row_ids = jnp.arange(rows, dtype=jnp.int32)
    segment, positions = locate(row_ids, seq_lengths[0])
    cos_table, sin_table = rope_tables(positions, head_width)
    own_queries = lambda array: (
        array if parts == 1 else lax.dynamic_slice_in_dim(array, query_start, query_count, 0)
    )
    query_ids = own_queries(row_ids)
    query_seg = own_queries(segment)
    query_cos = own_queries(cos_table)
    query_sin = own_queries(sin_table)
    allowed = window_mask(query_ids, query_seg, row_ids, segment)
    score_scale = head_width ** (-0.5)
    unit_in = resid_in * rms_factor(resid_in)
    normed_in = (unit_in * gain_in).astype(bf16)
    qkv = fdot(normed_in, qkv_w)
    query_raw = own_queries(qkv[:, :head_width])
    key_raw = qkv[:, head_width : 2 * head_width]
    value_bf = qkv[:, 2 * head_width :].astype(bf16)
    factor_q = rms_factor(query_raw)
    unit_q = query_raw * factor_q
    factor_k = rms_factor(key_raw)
    unit_k = key_raw * factor_k
    query_rot = rotate(unit_q * gain_q, query_cos, query_sin).astype(bf16)
    key_rot = rotate(unit_k * gain_k, cos_table, sin_table).astype(bf16)
    scores = jnp.where(allowed, times_transposed(query_rot, key_rot) * score_scale, NEG_FILL)
    row_max = jnp.max(scores, axis=-1, keepdims=True)
    log_total = row_max + jnp.log(jnp.sum(jnp.exp(scores - row_max), axis=-1, keepdims=True))
    probs = jnp.exp(scores - log_total)
    probs_bf = probs.astype(bf16)
    attended_own = fdot(probs_bf, value_bf).astype(bf16)
    attended_heads = gather_blocks(attended_own).reshape(num_heads, rows, head_width)
    attended = jnp.concatenate([attended_heads[i] for i in range(num_heads)], axis=1)
    attn_proj = fdot(attended, out_w)
    factor_pa = rms_factor(attn_proj)
    unit_pa = attn_proj * factor_pa
    hidden = resid_in + unit_pa * gain_pa
    factor_hid = rms_factor(hidden)
    unit_hid = hidden * factor_hid
    normed_ff = (unit_hid * gain_pf).astype(bf16)

    own_rows = lambda array: lax.dynamic_slice_in_dim(array, own * rows_here, rows_here, 0)
    rows_of = lambda array: (
        lambda peer: lax.dynamic_slice_in_dim(array, peer * rows_here, rows_here, 0)
    )
    far_normed = other_groups(own_rows(normed_ff), rows_of(normed_ff))

    gate_proj = fdot(normed_ff, gate_w)
    up_proj = fdot(normed_ff, up_w)
    gelu_value, gelu_slope = gelu_parts(gate_proj)
    mixed = (gelu_value * up_proj).astype(bf16)
    ff_proj = sum_to_owner(fdot(mixed, w_down))
    hidden_own = own_rows(hidden)
    factor_ff = rms_factor(ff_proj)
    unit_ff = ff_proj * factor_ff
    block_out = (hidden_own + unit_ff * gain_pff).astype(bf16)
    grad_out = cotangent[0].astype(f32)
    grad_gain_pff = jnp.sum(grad_out * unit_ff, axis=0)
    grad_ff_own = norm_back(grad_out * gain_pff, unit_ff, factor_ff).astype(bf16)
    grad_ff_proj = gather_blocks(grad_ff_own).reshape(rows, width)
    far_grad_ff = other_groups(grad_ff_own, rows_of(grad_ff_proj))
    grad_mixed = times_transposed(grad_ff_proj, w_down)
    grad_gate = (grad_mixed * up_proj * gelu_slope).astype(bf16)
    grad_up = (grad_mixed * gelu_value).astype(bf16)
    grad_normed_ff = sum_to_owner(
        times_transposed(grad_gate, gate_w) + times_transposed(grad_up, up_w)
    )
    factor_hid_own = own_rows(factor_hid)
    unit_hid_own = hidden_own * factor_hid_own
    grad_gain_pf = jnp.sum(grad_normed_ff * unit_hid_own, axis=0)
    grad_hidden = grad_out + norm_back(grad_normed_ff * gain_pf, unit_hid_own, factor_hid_own)
    factor_pa_own = own_rows(factor_pa)
    unit_pa_own = own_rows(attn_proj) * factor_pa_own
    grad_gain_pa = jnp.sum(grad_hidden * unit_pa_own, axis=0)
    grad_attn_own = norm_back(grad_hidden * gain_pa, unit_pa_own, factor_pa_own).astype(bf16)
    grad_attn_proj = gather_blocks(grad_attn_own).reshape(rows, width)

    far_gate = fdot(far_normed, gate_w)
    far_up = fdot(far_normed, up_w)
    far_value, far_slope = gelu_parts(far_gate)
    far_mixed = (far_value * far_up).astype(bf16)
    far_grad_mixed = times_transposed(far_grad_ff, w_down)
    far_grad_gate = (far_grad_mixed * far_up * far_slope).astype(bf16)
    far_grad_up = (far_grad_mixed * far_value).astype(bf16)
    down_grad = outer_sum(mixed, grad_ff_proj) + outer_sum(far_mixed, far_grad_ff)
    gate_grad = outer_sum(normed_ff, grad_gate) + outer_sum(far_normed, far_grad_gate)
    up_grad = outer_sum(normed_ff, grad_up) + outer_sum(far_normed, far_grad_up)
    down_half = sum_over_cores(down_grad.reshape(2, columns // 2, width), core)
    share_down = join_halves(down_half, core, 0).reshape(columns, width).astype(f32)

    def split_rows(grad):
        halves = grad.reshape(peers, 2, half_rows, columns).swapaxes(0, 1)
        part = sum_over_cores(halves, core)
        received = in_order(exchange_blocks(lambda peer: pick(part, peer)))
        whole = join_halves(received, core, 1).reshape(peers, slice_rows, columns)
        return jnp.concatenate([whole[i] for i in range(peers)], axis=1).astype(f32)

    share_gate = split_rows(gate_grad)
    share_up = split_rows(up_grad)

    out_head = lax.dynamic_slice_in_dim(out_w, head * head_width, head_width, 0)
    attended_cols = lax.dynamic_slice_in_dim(attended, own * out_rows, out_rows, 1)
    if parts == 1:
        out_head = w_out
        attended_cols = attended_own
    out_grad = outer_sum(attended_cols, grad_attn_proj)
    grad_attended = times_transposed(own_queries(grad_attn_proj), out_head).astype(bf16)
    grad_probs = times_transposed(grad_attended, value_bf)
    delta = jnp.sum(
        grad_attended.astype(f32) * attended_own.astype(f32), axis=-1, keepdims=True
    )
    grad_scores = (probs * (grad_probs - delta) * score_scale).astype(bf16)
    grad_value = outer_sum(probs_bf, grad_attended).astype(bf16)
    grad_key_rot = outer_sum(grad_scores, query_rot)
    grad_query_rot = fdot(grad_scores, key_rot)
    grad_unit_q = unrotate(grad_query_rot, query_cos, query_sin)
    grad_unit_k = unrotate(grad_key_rot, cos_table, sin_table)
    grad_gain_q = jnp.sum(grad_unit_q * unit_q, axis=0)
    grad_gain_k = jnp.sum(grad_unit_k * unit_k, axis=0)
    grad_query = norm_back(grad_unit_q * gain_q, unit_q, factor_q).astype(bf16)
    grad_key = norm_back(grad_unit_k * gain_k, unit_k, factor_k).astype(bf16)
    if parts > 1:
        grad_query = lax.dynamic_update_slice_in_dim(
            jnp.zeros((rows, head_width), bf16), grad_query, query_start, 0
        )
    grad_qkv = jnp.concatenate([grad_query, grad_key, grad_value], axis=1)
    grad_normed_in = sum_to_owner(times_transposed(grad_qkv, qkv_w))
    qkv_grad = outer_sum(normed_in, grad_qkv)
    resid_own = block_in[0].astype(f32)
    factor_in_own = rms_factor(resid_own)
    unit_in_own = resid_own * factor_in_own
    grad_gain_in = jnp.sum(grad_normed_in * unit_in_own, axis=0)
    grad_input = (
        grad_hidden + norm_back(grad_normed_in * gain_in, unit_in_own, factor_in_own)
    ).astype(bf16)

    gain_grads = (
        grad_gain_in,
        grad_gain_pa,
        grad_gain_pf,
        grad_gain_pff,
        grad_gain_q,
        grad_gain_k,
    )
    gain_sums = jnp.concatenate([part.reshape(peers, -1) for part in gain_grads], axis=1)
    gain_count = gain_sums.shape[1] // 2
    gain_sums = jnp.pad(
        gain_sums.reshape(peers, 2, 1, gain_count),
        ((0, 0), (0, 0), (0, 15), (0, 3 * head_width - gain_count)),
    )
    attn_grads = jnp.concatenate(
        [qkv_grad.reshape(peers, 2, half_rows, 3 * head_width), gain_sums], axis=2
    )
    attn_half = sum_over_cores(attn_grads.swapaxes(0, 1), core)
    received = in_order(exchange_blocks(lambda peer: pick(attn_half, peer))).astype(f32)
    heads_sum = received[:, :half_rows, :head_width].reshape(
        num_heads, parts, half_rows, head_width
    )
    heads_sum = jnp.sum(heads_sum, axis=1)
    query_part = jnp.concatenate([heads_sum[i] for i in range(num_heads)], axis=1)
    rest = jnp.sum(received, axis=0)
    kv_part = rest[:half_rows, head_width:]
    out_half = sum_over_cores(out_grad.reshape(2, out_rows // 2, width), core)
    qkv_half = jnp.concatenate([query_part, kv_part], axis=1).astype(bf16)
    gain_half = rest[half_rows:].astype(bf16)
    qkv_rows = qkv_half.size // width
    half_out = out_rows // 2
    gain_pad = jnp.pad(gain_half[0], (0, 16 * width - gain_half.shape[1])).reshape(16, width)
    small = sum_over_pairs(
        jnp.concatenate([qkv_half.reshape(qkv_rows, width), out_half, gain_pad], axis=0)
    )
    small = join_halves(small, core, 0).astype(f32)
    share_qkv = small[:, :qkv_rows].reshape(slice_rows, (num_heads + 2) * head_width)
    query_width = num_heads * head_width
    share_query = share_qkv[:, :query_width]
    share_key = share_qkv[:, query_width : query_width + head_width]
    share_value = share_qkv[:, query_width + head_width :]
    share_out = small[:, qkv_rows : qkv_rows + half_out].reshape(out_rows, width)
    gain_line = small[:, qkv_rows + half_out, :gain_count].reshape(-1)
    sections = [slice_rows, slice_rows, slice_rows, slice_rows, gain_slice, gain_slice]
    shares = []
    start = 0
    for size in sections:
        shares.append(gain_line[start : start + size])
        start = start + size
    share_in, share_pa, share_pf, share_pff, share_q, share_k = shares
    return (
        block_out[None],
        grad_input[None],
        share_in,
        share_query,
        share_key,
        share_value,
        share_q,
        share_k,
        share_out,
        share_pa,
        share_pf,
        share_gate,
        share_up,
        share_down,
        share_pff,
    )


def solution(mesh):
    placed = (
        P("rep", "fsdp", None),
        P("rep", None),
        P("fsdp"),
        P("fsdp", None),
        P("fsdp", None),
        P("fsdp", None),
        P("fsdp"),
        P("fsdp"),
        P("fsdp", None),
        P("fsdp"),
        P("fsdp"),
        P("fsdp", None),
        P("fsdp", None),
        P("fsdp", None),
        P("fsdp"),
        P("rep", "fsdp", None),
    )
    return jax.shard_map(
        body,
        mesh=mesh,
        in_specs=placed,
        out_specs=(
            P("rep", "fsdp", None),
            P("rep", "fsdp", None),
            P("fsdp"),
            P("fsdp", None),
            P("fsdp", None),
            P("fsdp", None),
            P("fsdp"),
            P("fsdp"),
            P("fsdp", None),
            P("fsdp"),
            P("fsdp"),
            P("fsdp", None),
            P("fsdp", None),
            P("fsdp", None),
            P("fsdp"),
        ),
        check_vma=False,
    )
```

```python
import math

import jax
import jax.numpy as jnp
from jax import lax
from jax.experimental import pallas as pl
from jax.experimental.pallas import tpu as pltpu
from jax.sharding import PartitionSpec as P

WINDOW = 512


EPSILON = 1e-06
NEG_FILL = -1e30
GELU_SCALE = math.sqrt(2.0 / math.pi)


def swap_cores(block):
    return lax.ppermute(block, "rep", [(i, i ^ 1) for i in range(lax.axis_size("rep"))])


def to_peer(block, step):
    return lax.ppermute(block, "fsdp", [(i, i ^ step) for i in range(lax.axis_size("fsdp"))])


def pick(blocks, index, axis=0):
    return lax.dynamic_index_in_dim(blocks, index, axis, keepdims=False)


def copy_blocks(blocks, out_shapes, target):
    count = len(blocks)

    def kernel(*refs):
        outputs = refs[count:-1]
        copies = []
        for i in range(count):
            copy = pltpu.make_async_copy(refs[i], target(i, outputs), refs[-1].at[i])
            copy.start()
            copies.append(copy)
        for copy in copies:
            copy.wait()

    return pl.pallas_call(
        kernel,
        out_shape=out_shapes,
        in_specs=[pl.BlockSpec(memory_space=pl.ANY)] * count,
        out_specs=[pl.BlockSpec(memory_space=pl.ANY)] * len(out_shapes),
        scratch_shapes=[pltpu.SemaphoreType.DMA((count,))],
    )(*blocks)


def gather_blocks(block):
    peers = lax.axis_size("fsdp")
    received = [block] + [to_peer(block, step) for step in range(1, peers)]
    shape = jax.ShapeDtypeStruct((peers,) + block.shape, block.dtype)
    return copy_blocks(
        received, [shape], lambda i, outputs: outputs[0].at[lax.axis_index("fsdp") ^ i]
    )[0]


def exchange_blocks(block_for):
    own = lax.axis_index("fsdp")
    peers = lax.axis_size("fsdp")
    return [block_for(own)] + [to_peer(block_for(own ^ step), step) for step in range(1, peers)]


def place_halves(received):
    peers = len(received)
    blocks = received + [swap_cores(block) for block in received]
    shape = jax.ShapeDtypeStruct((peers, 2) + received[0].shape, received[0].dtype)

    def target(i, outputs):
        half = (lax.axis_index("rep") + i // peers) % 2
        return outputs[0].at[lax.axis_index("fsdp") ^ (i % peers), half]

    return copy_blocks(blocks, [shape], target)[0]


def place_pairs(received):
    peers = len(received)
    blocks = received + [swap_cores(block) for block in received]
    shape = jax.ShapeDtypeStruct((peers, 2) + received[0].shape[1:], received[0].dtype)

    def target(i, outputs):
        half = (lax.axis_index("rep") + (i // 2) // peers) % 2
        return outputs[i % 2].at[lax.axis_index("fsdp") ^ ((i // 2) % peers), half]

    return copy_pairs(blocks, [shape, shape], target)


def copy_pairs(blocks, out_shapes, target):
    count = 2 * len(blocks)

    def kernel(*refs):
        outputs = refs[len(blocks) : -1]
        copies = []
        for i in range(count):
            source = refs[i // 2].at[i % 2]
            copy = pltpu.make_async_copy(source, target(i, outputs), refs[-1].at[i])
            copy.start()
            copies.append(copy)
        for copy in copies:
            copy.wait()

    return pl.pallas_call(
        kernel,
        out_shape=out_shapes,
        in_specs=[pl.BlockSpec(memory_space=pl.ANY)] * len(blocks),
        out_specs=[pl.BlockSpec(memory_space=pl.ANY)] * 2,
        scratch_shapes=[pltpu.SemaphoreType.DMA((count,))],
    )(*blocks)


def widen_rows(received):
    peers = len(received)
    half_rows, columns = received[0].shape
    others = [swap_cores(block) for block in received]
    chunk = half_rows // 3 if half_rows % 48 == 0 else half_rows
    steps = half_rows // chunk

    def kernel(*refs):
        own = lax.axis_index("fsdp")
        core = lax.axis_index("rep") % 2
        mine = pl.program_id(0) == core
        out = refs[-1]
        for i in range(peers):
            for k in range(peers):

                @pl.when((own ^ k) == i)
                def _():
                    block = jnp.where(mine, refs[k][...], refs[peers + k][...])
                    out[:, i * columns : (i + 1) * columns] = block.astype(jnp.float32)

    return pl.pallas_call(
        kernel,
        grid=(2, steps),
        out_shape=jax.ShapeDtypeStruct((2 * half_rows, peers * columns), jnp.float32),
        in_specs=[pl.BlockSpec((chunk, columns), lambda h, i: (i, 0))] * (2 * peers),
        out_specs=pl.BlockSpec((chunk, peers * columns), lambda h, i: (h * steps + i, 0)),
    )(*received, *others)


def join_halves(mine, core):
    other = swap_cores(mine)
    first = core == 0
    return jnp.stack([jnp.where(first, mine, other), jnp.where(first, other, mine)])


def sum_to_owner(partial):
    own = lax.axis_index("fsdp")
    peers = lax.axis_size("fsdp")
    blocks = partial.reshape((peers, partial.shape[0] // peers) + partial.shape[1:])
    total = pick(blocks, own)
    for step in range(1, peers):
        sent = pick(blocks, own ^ step).astype(jnp.bfloat16)
        total = total + to_peer(sent, step).astype(jnp.float32)
    return total


def sum_over_cores(halves, core, axis=0):
    mine = pick(halves, core, axis)
    other = swap_cores(pick(halves, 1 - core, axis).astype(jnp.bfloat16))
    return (mine + other.astype(jnp.float32)).astype(jnp.bfloat16)


def add_rounded(first_op, second_op):
    return (first_op.astype(jnp.float32) + second_op.astype(jnp.float32)).astype(jnp.bfloat16)


def along_line(block, moves):
    pairs = [(2 * i + core, 2 * j + core) for i, j in moves for core in (0, 1)]
    return lax.ppermute(block, "rep", pairs)


def sum_over_pairs(block):
    pairs = lax.axis_size("rep") // 2
    if pairs != 4:
        step = 1
        while step < pairs:
            block = add_rounded(block, along_line(block, [(i, i ^ step) for i in range(pairs)]))
            step = 2 * step
        return block
    pair = lax.axis_index("rep") // 2
    inner = (pair == 1) | (pair == 2)
    block = add_rounded(block, along_line(block, [(0, 1), (3, 2)]))
    block = add_rounded(block, along_line(block, [(1, 2), (2, 1)]))
    return jnp.where(inner, block, along_line(block, [(1, 0), (2, 3)]))


def across_pairs(block):
    pairs = lax.axis_size("rep") // 2
    return [along_line(block, [(i, i ^ step) for i in range(pairs)]) for step in range(1, pairs)]


def send_across(own_rows, rows_of):
    if lax.axis_size("fsdp") != 4:
        return jnp.stack(across_pairs(own_rows))
    sent = jnp.stack([own_rows, rows_of(lax.axis_index("fsdp") ^ 3)])
    return jnp.stack(across_pairs(sent), 1)


def spread_rows(received):
    width = received.shape[-1]
    if lax.axis_size("fsdp") != 4:
        return gather_blocks(received).reshape(-1, width)
    near = [to_peer(received[0], step) for step in (1, 2)]
    return jnp.concatenate([received.reshape(-1, width)] + [x.reshape(-1, width) for x in near])


def rms_factor(values):
    return lax.rsqrt(jnp.mean(values * values, axis=-1, keepdims=True) + EPSILON)


def norm_back(grad_unit, unit_vals, factor):
    return factor * (
        grad_unit - unit_vals * jnp.mean(grad_unit * unit_vals, axis=-1, keepdims=True)
    )


def gelu_parts(values):
    cubic = values * values * values
    tangent = jnp.tanh(GELU_SCALE * (values + 0.044715 * cubic))
    result = 0.5 * values * (1.0 + tangent)
    slope = 0.5 * (1.0 + tangent) + 0.5 * values * (1.0 - tangent * tangent) * GELU_SCALE * (
        1.0 + 3.0 * 0.044715 * values * values
    )
    return (result, slope)


def rope_tables(positions, head_width):
    half_width = head_width // 2
    freqs = 10000.0 ** (-2.0 * jnp.arange(half_width, dtype=jnp.float32) / head_width)
    angles = positions.astype(jnp.float32)[:, None] * freqs[None, :]
    return (jnp.cos(angles), jnp.sin(angles))


def rotate(values, cos_table, sin_table):
    half_width = values.shape[-1] // 2
    lower_half = values[..., :half_width]
    upper_half = values[..., half_width:]
    return jnp.concatenate(
        [
            lower_half * cos_table - upper_half * sin_table,
            upper_half * cos_table + lower_half * sin_table,
        ],
        axis=-1,
    )


def unrotate(grads, cos_table, sin_table):
    half_width = grads.shape[-1] // 2
    lower_half = grads[..., :half_width]
    upper_half = grads[..., half_width:]
    return jnp.concatenate(
        [
            lower_half * cos_table + upper_half * sin_table,
            upper_half * cos_table - lower_half * sin_table,
        ],
        axis=-1,
    )


def locate(row_ids, lengths):
    ends = jnp.cumsum(lengths)
    starts = ends - lengths
    segment = jnp.sum((row_ids[:, None] >= ends[None, :]).astype(jnp.int32), axis=1)
    choose = segment[:, None] == jnp.arange(lengths.shape[0], dtype=jnp.int32)[None, :]
    first_row = jnp.sum(jnp.where(choose, starts[None, :], 0), axis=1)
    return (segment, row_ids - first_row)


def window_mask(query_rows, query_seg, key_rows, key_seg):
    distance = query_rows[:, None] - key_rows[None, :]
    return (
        (query_seg[:, None] == key_seg[None, :])
        & (distance >= 0)
        & (distance < WINDOW)
        & (key_rows[None, :] >= 0)
    )


def fdot(first_op, second_op):
    return jnp.dot(first_op, second_op, preferred_element_type=jnp.float32)


def times_transposed(first_op, second_op):
    return lax.dot_general(
        first_op, second_op, (((1,), (1,)), ((), ())), preferred_element_type=jnp.float32
    )


def outer_sum(first_op, second_op):
    return lax.dot_general(
        first_op, second_op, (((0,), (0,)), ((), ())), preferred_element_type=jnp.float32
    )


def body(
    block_in,
    seq_lengths,
    input_gain,
    w_query,
    w_key,
    w_value,
    query_gain,
    key_gain,
    w_out,
    post_attn_gain,
    pre_ff_gain,
    w_gate,
    w_up,
    w_down,
    post_ff_gain,
    cotangent,
):
    bf16 = jnp.bfloat16
    f32 = jnp.float32
    own = lax.axis_index("fsdp")
    peers = lax.axis_size("fsdp")
    core = lax.axis_index("rep") % 2
    rows_here, width = block_in.shape[1:]
    rows = rows_here * peers
    head_width = w_key.shape[1]
    num_heads = w_query.shape[1] // head_width
    parts = peers // num_heads
    query_count = rows // parts
    head = own // parts
    query_start = (own % parts) * query_count
    slice_rows = w_gate.shape[0]
    half_rows = slice_rows // 2
    columns = w_down.shape[0]
    out_rows = w_out.shape[0]
    gain_slice = query_gain.shape[0]

    resid_in = gather_blocks(block_in[0]).reshape(rows, width).astype(f32)

    half_of = lambda matrix: pick(matrix.reshape(2, matrix.shape[0] // 2, matrix.shape[1]), core)
    gain_parts = (input_gain, post_attn_gain, pre_ff_gain, post_ff_gain, query_gain, key_gain)
    gain_line = jnp.concatenate(gain_parts)
    gain_width = 3 * head_width
    gain_block = jnp.pad(gain_line, (0, 16 * gain_width - gain_line.shape[0]))
    gain_block = gain_block.reshape(16, gain_width)
    query_half = half_of(w_query)
    kv_half = jnp.concatenate([half_of(w_key), half_of(w_value)], axis=1)

    def attn_block(peer):
        mine = lax.dynamic_slice_in_dim(query_half, (peer // parts) * head_width, head_width, 1)
        return jnp.concatenate([jnp.concatenate([mine, kv_half], axis=1), gain_block])

    qkv_blocks = exchange_blocks(attn_block)
    qkv_blocks, out_half = lax.optimization_barrier((qkv_blocks, half_of(w_out)))
    qkv_all = place_halves(qkv_blocks)
    qkv_w = qkv_all[:, :, :half_rows].reshape(width, gain_width)
    gain_lines = qkv_all[:, 0, half_rows : half_rows + 2].reshape(peers, 2 * gain_width).astype(f32)
    gains = []
    start = 0
    for part in gain_parts:
        gains.append(gain_lines[:, start : start + part.shape[0]].reshape(-1))
        start = start + part.shape[0]
    gain_in, gain_pa, gain_pf, gain_pff, gain_q, gain_k = gains
    out_blocks = [out_half] + [to_peer(out_half, step) for step in range(1, peers)]
    out_w = place_halves(out_blocks).reshape(-1, width)

    gate_half = half_of(w_gate)
    up_half = half_of(w_up)

    def ff_block(peer):
        first = lax.dynamic_slice_in_dim(gate_half, peer * columns, columns, 1)
        second = lax.dynamic_slice_in_dim(up_half, peer * columns, columns, 1)
        return jnp.stack([first, second])

    ff_sent = [ff_block(own ^ step) for step in range(peers)]
    qkv_blocks, ff_sent = lax.optimization_barrier((qkv_blocks, ff_sent))
    ff_blocks = [ff_sent[0]] + [to_peer(ff_sent[step], step) for step in range(1, peers)]
    gate_w, up_w = [whole.reshape(width, columns) for whole in place_pairs(ff_blocks)]

    row_ids = jnp.arange(rows, dtype=jnp.int32)
    segment, positions = locate(row_ids, seq_lengths[0])
    cos_table, sin_table = rope_tables(positions, head_width)
    own_queries = lambda array: (
        array if parts == 1 else lax.dynamic_slice_in_dim(array, query_start, query_count, 0)
    )
    query_ids = own_queries(row_ids)
    query_seg = own_queries(segment)
    query_cos = own_queries(cos_table)
    query_sin = own_queries(sin_table)
    allowed = window_mask(query_ids, query_seg, row_ids, segment)
    score_scale = head_width ** (-0.5)
    unit_in = resid_in * rms_factor(resid_in)
    normed_in = (unit_in * gain_in).astype(bf16)
    qkv = fdot(normed_in, qkv_w)
    query_raw = own_queries(qkv[:, :head_width])
    key_raw = qkv[:, head_width : 2 * head_width]
    value_bf = qkv[:, 2 * head_width :].astype(bf16)
    factor_q = rms_factor(query_raw)
    unit_q = query_raw * factor_q
    factor_k = rms_factor(key_raw)
    unit_k = key_raw * factor_k
    query_rot = rotate(unit_q * gain_q, query_cos, query_sin).astype(bf16)
    key_rot = rotate(unit_k * gain_k, cos_table, sin_table).astype(bf16)
    scores = jnp.where(allowed, times_transposed(query_rot, key_rot) * score_scale, NEG_FILL)
    row_max = jnp.max(scores, axis=-1, keepdims=True)
    log_total = row_max + jnp.log(jnp.sum(jnp.exp(scores - row_max), axis=-1, keepdims=True))
    probs = jnp.exp(scores - log_total)
    probs_bf = probs.astype(bf16)
    attended_own = fdot(probs_bf, value_bf).astype(bf16)
    attended_blocks = [attended_own] + [to_peer(attended_own, step) for step in range(1, peers)]

    def attended_window(i, outputs):
        peer = lax.axis_index("fsdp") ^ i
        first_row = pl.multiple_of((peer % parts) * query_count, query_count)
        first_column = pl.multiple_of((peer // parts) * head_width, head_width)
        return outputs[0].at[pl.ds(first_row, query_count), pl.ds(first_column, head_width)]

    attended = copy_blocks(
        attended_blocks,
        [jax.ShapeDtypeStruct((rows, num_heads * head_width), bf16)],
        attended_window,
    )[0]
    attn_proj = fdot(attended, out_w)
    factor_pa = rms_factor(attn_proj)
    unit_pa = attn_proj * factor_pa
    hidden = resid_in + unit_pa * gain_pa
    factor_hid = rms_factor(hidden)
    unit_hid = hidden * factor_hid
    normed_ff = (unit_hid * gain_pf).astype(bf16)

    own_rows = lambda array: lax.dynamic_slice_in_dim(array, own * rows_here, rows_here, 0)
    rows_of = lambda array: (
        lambda peer: lax.dynamic_slice_in_dim(array, peer * rows_here, rows_here, 0)
    )
    far_normed = send_across(own_rows(normed_ff), rows_of(normed_ff))

    def forward_factors(rows_in):
        gate_proj = fdot(rows_in, gate_w)
        up_proj = fdot(rows_in, up_w)
        gelu_value, gelu_slope = gelu_parts(gate_proj)
        mixed = (gelu_value * up_proj).astype(bf16)
        factors = (mixed, (up_proj * gelu_slope).astype(bf16), gelu_value.astype(bf16))
        return lax.optimization_barrier(factors)

    def backward_factors(grad_rows, slope_up, value):
        grad_mixed = times_transposed(grad_rows, w_down)
        grad_gate = (grad_mixed * slope_up.astype(f32)).astype(bf16)
        grad_up = (grad_mixed * value.astype(f32)).astype(bf16)
        return lax.optimization_barrier((grad_gate, grad_up))

    mixed, slope_up, value_ff = forward_factors(normed_ff)
    ff_proj = sum_to_owner(fdot(mixed, w_down))
    hidden_own = own_rows(hidden)
    factor_ff = rms_factor(ff_proj)
    unit_ff = ff_proj * factor_ff
    block_out = (hidden_own + unit_ff * gain_pff).astype(bf16)
    grad_out = cotangent[0].astype(f32)
    grad_gain_pff = jnp.sum(grad_out * unit_ff, axis=0)
    grad_ff_own = norm_back(grad_out * gain_pff, unit_ff, factor_ff).astype(bf16)
    grad_ff_proj = gather_blocks(grad_ff_own).reshape(rows, width)
    far_grad_ff = send_across(grad_ff_own, rows_of(grad_ff_proj))
    grad_gate, grad_up = backward_factors(grad_ff_proj, slope_up, value_ff)
    grad_normed_part = times_transposed(grad_gate, gate_w) + times_transposed(grad_up, up_w)
    grad_normed_part, far_normed = lax.optimization_barrier((grad_normed_part, far_normed))
    grad_normed_ff = sum_to_owner(grad_normed_part)
    far_normed = spread_rows(far_normed)
    factor_hid_own = own_rows(factor_hid)
    unit_hid_own = hidden_own * factor_hid_own
    grad_gain_pf = jnp.sum(grad_normed_ff * unit_hid_own, axis=0)
    grad_hidden = grad_out + norm_back(grad_normed_ff * gain_pf, unit_hid_own, factor_hid_own)
    factor_pa_own = own_rows(factor_pa)
    unit_pa_own = own_rows(attn_proj) * factor_pa_own
    grad_gain_pa = jnp.sum(grad_hidden * unit_pa_own, axis=0)
    grad_attn_own = norm_back(grad_hidden * gain_pa, unit_pa_own, factor_pa_own).astype(bf16)
    grad_attn_proj = gather_blocks(grad_attn_own).reshape(rows, width)

    far_mixed, far_slope_up, far_value = forward_factors(far_normed)
    grad_attn_proj, far_grad_ff = lax.optimization_barrier((grad_attn_proj, far_grad_ff))
    far_grad_ff = spread_rows(far_grad_ff)
    far_grad_gate, far_grad_up = backward_factors(far_grad_ff, far_slope_up, far_value)
    gate_grad = outer_sum(normed_ff, grad_gate) + outer_sum(far_normed, far_grad_gate)
    up_grad = outer_sum(normed_ff, grad_up) + outer_sum(far_normed, far_grad_up)
    down_grad = outer_sum(mixed, grad_ff_proj) + outer_sum(far_mixed, far_grad_ff)
    down_half = sum_over_cores(down_grad.reshape(2, columns // 2, width), core)
    share_down = join_halves(down_half, core).reshape(columns, width).astype(f32)

    def split_rows(grad):
        part = sum_over_cores(grad.reshape(peers, 2, half_rows, columns), core, 1)
        return widen_rows(exchange_blocks(lambda peer: pick(part, peer)))

    share_gate = split_rows(gate_grad)
    share_up = split_rows(up_grad)

    out_head = lax.dynamic_slice_in_dim(out_w, head * head_width, head_width, 0)
    attended_cols = lax.dynamic_slice_in_dim(attended, own * out_rows, out_rows, 1)
    if parts == 1:
        out_head = w_out
        attended_cols = attended_own
    out_grad = outer_sum(attended_cols, grad_attn_proj)
    grad_attended = times_transposed(own_queries(grad_attn_proj), out_head).astype(bf16)
    grad_probs = times_transposed(grad_attended, value_bf)
    delta = jnp.sum(
        grad_attended.astype(f32) * attended_own.astype(f32), axis=-1, keepdims=True
    )
    grad_scores = (probs * (grad_probs - delta) * score_scale).astype(bf16)
    grad_value = outer_sum(probs_bf, grad_attended).astype(bf16)
    grad_key_rot = outer_sum(grad_scores, query_rot)
    grad_query_rot = fdot(grad_scores, key_rot)
    grad_unit_q = unrotate(grad_query_rot, query_cos, query_sin)
    grad_unit_k = unrotate(grad_key_rot, cos_table, sin_table)
    grad_gain_q = jnp.sum(grad_unit_q * unit_q, axis=0)
    grad_gain_k = jnp.sum(grad_unit_k * unit_k, axis=0)
    grad_query = norm_back(grad_unit_q * gain_q, unit_q, factor_q).astype(bf16)
    grad_key = norm_back(grad_unit_k * gain_k, unit_k, factor_k).astype(bf16)
    if parts > 1:
        grad_query = lax.dynamic_update_slice_in_dim(
            jnp.zeros((rows, head_width), bf16), grad_query, query_start, 0
        )
    grad_qkv = jnp.concatenate([grad_query, grad_key, grad_value], axis=1)
    grad_normed_in = sum_to_owner(times_transposed(grad_qkv, qkv_w))
    qkv_grad = outer_sum(normed_in, grad_qkv)
    resid_own = block_in[0].astype(f32)
    factor_in_own = rms_factor(resid_own)
    unit_in_own = resid_own * factor_in_own
    grad_gain_in = jnp.sum(grad_normed_in * unit_in_own, axis=0)
    grad_input = (
        grad_hidden + norm_back(grad_normed_in * gain_in, unit_in_own, factor_in_own)
    ).astype(bf16)

    gain_grads = (
        grad_gain_in,
        grad_gain_pa,
        grad_gain_pf,
        grad_gain_pff,
        grad_gain_q,
        grad_gain_k,
    )
    gain_sums = jnp.concatenate([part.reshape(peers, -1) for part in gain_grads], axis=1)
    gain_count = gain_sums.shape[1] // 2
    gain_sums = jnp.pad(
        gain_sums.reshape(peers, 2, 1, gain_count),
        ((0, 0), (0, 0), (0, 15), (0, 3 * head_width - gain_count)),
    )
    attn_grads = jnp.concatenate(
        [qkv_grad.reshape(peers, 2, half_rows, 3 * head_width), gain_sums], axis=2
    )
    attn_half = sum_over_cores(attn_grads, core, 1)
    received = exchange_blocks(lambda peer: pick(attn_half, peer))
    received = copy_blocks(
        received,
        [jax.ShapeDtypeStruct((peers,) + received[0].shape, bf16)],
        lambda i, outputs: outputs[0].at[lax.axis_index("fsdp") ^ i],
    )[0].astype(f32)
    heads_sum = received[:, :half_rows, :head_width].reshape(
        num_heads, parts, half_rows, head_width
    )
    heads_sum = jnp.sum(heads_sum, axis=1)
    query_part = jnp.concatenate([heads_sum[i] for i in range(num_heads)], axis=1)
    rest = jnp.sum(received, axis=0)
    kv_part = rest[:half_rows, head_width:]
    out_half = sum_over_cores(out_grad.reshape(2, out_rows // 2, width), core)
    qkv_half = jnp.concatenate([query_part, kv_part], axis=1).astype(bf16)
    gain_half = rest[half_rows:].astype(bf16)
    qkv_rows = qkv_half.size // width
    half_out = out_rows // 2
    gain_pad = jnp.pad(gain_half[0], (0, 16 * width - gain_half.shape[1])).reshape(16, width)
    small = sum_over_pairs(
        jnp.concatenate([qkv_half.reshape(qkv_rows, width), out_half, gain_pad], axis=0)
    )
    small = join_halves(small, core).astype(f32)
    share_qkv = small[:, :qkv_rows].reshape(slice_rows, (num_heads + 2) * head_width)
    query_width = num_heads * head_width
    share_query = share_qkv[:, :query_width]
    share_key = share_qkv[:, query_width : query_width + head_width]
    share_value = share_qkv[:, query_width + head_width :]
    share_out = small[:, qkv_rows : qkv_rows + half_out].reshape(out_rows, width)
    gain_line = small[:, qkv_rows + half_out, :gain_count].reshape(-1)
    sections = [slice_rows, slice_rows, slice_rows, slice_rows, gain_slice, gain_slice]
    shares = []
    start = 0
    for size in sections:
        shares.append(gain_line[start : start + size])
        start = start + size
    share_in, share_pa, share_pf, share_pff, share_q, share_k = shares
    return (
        block_out[None],
        grad_input[None],
        share_in,
        share_query,
        share_key,
        share_value,
        share_q,
        share_k,
        share_out,
        share_pa,
        share_pf,
        share_gate,
        share_up,
        share_down,
        share_pff,
    )


def solution(mesh):
    placed = (
        P("rep", "fsdp", None),
        P("rep", None),
        P("fsdp"),
        P("fsdp", None),
        P("fsdp", None),
        P("fsdp", None),
        P("fsdp"),
        P("fsdp"),
        P("fsdp", None),
        P("fsdp"),
        P("fsdp"),
        P("fsdp", None),
        P("fsdp", None),
        P("fsdp", None),
        P("fsdp"),
        P("rep", "fsdp", None),
    )
    return jax.shard_map(
        body,
        mesh=mesh,
        in_specs=placed,
        out_specs=(
            P("rep", "fsdp", None),
            P("rep", "fsdp", None),
            P("fsdp"),
            P("fsdp", None),
            P("fsdp", None),
            P("fsdp", None),
            P("fsdp"),
            P("fsdp"),
            P("fsdp", None),
            P("fsdp"),
            P("fsdp"),
            P("fsdp", None),
            P("fsdp", None),
            P("fsdp", None),
            P("fsdp"),
        ),
        check_vma=False,
    )
```

```python
import math

import jax
import jax.numpy as jnp
from jax import lax
from jax.experimental import pallas as pl
from jax.experimental.pallas import tpu as pltpu
from jax.sharding import PartitionSpec as P

WINDOW = 512


EPSILON = 1e-06
NEG_FILL = -1e30
GELU_SCALE = math.sqrt(2.0 / math.pi)


def swap_cores(block):
    return lax.ppermute(block, "rep", [(i, i ^ 1) for i in range(lax.axis_size("rep"))])


def to_peer(block, step):
    return lax.ppermute(block, "fsdp", [(i, i ^ step) for i in range(lax.axis_size("fsdp"))])


def pick(blocks, index, axis=0):
    return lax.dynamic_index_in_dim(blocks, index, axis, keepdims=False)


def copy_blocks(blocks, shape, store):
    count = len(blocks)

    def kernel(*refs):
        for i in range(count):
            store(i, refs[i][...], refs[-1])

    shape = jax.ShapeDtypeStruct(shape, blocks[0].dtype)
    return pl.pallas_call(kernel, out_shape=shape)(*blocks)


def peer_of(i):
    return lax.axis_index("fsdp") ^ i


def in_order(received):
    def store(i, value, output):
        output[peer_of(i)] = value

    return copy_blocks(received, (len(received),) + received[0].shape, store)


def gather_blocks(block):
    peers = lax.axis_size("fsdp")
    return in_order([block] + [to_peer(block, step) for step in range(1, peers)])


def exchange_blocks(block_for):
    own = lax.axis_index("fsdp")
    peers = lax.axis_size("fsdp")
    return [block_for(own)] + [to_peer(block_for(own ^ step), step) for step in range(1, peers)]


def place_halves(received):
    peers = len(received)
    blocks = received + [swap_cores(block) for block in received]

    def store(i, value, output):
        output[peer_of(i % peers), (lax.axis_index("rep") + i // peers) % 2] = value

    return copy_blocks(blocks, (peers, 2) + received[0].shape, store)


def place_pairs(received):
    peers = len(received)
    blocks = received + [swap_cores(block) for block in received]

    def kernel(*refs):
        for i in range(2 * peers):
            half = (lax.axis_index("rep") + i // peers) % 2
            refs[-2][peer_of(i % peers), half] = refs[i][0]
            refs[-1][peer_of(i % peers), half] = refs[i][1]

    shape = jax.ShapeDtypeStruct((peers, 2) + received[0].shape[1:], received[0].dtype)
    return pl.pallas_call(kernel, out_shape=[shape, shape])(*blocks)


def whole_block(shape):
    return pl.BlockSpec(shape, lambda i: (0,) * len(shape), pipeline_mode=pl.Buffered(1))


def row_block(rows, columns):
    return pl.BlockSpec((rows, columns), lambda i: (i, 0))


def forward_factors(rows_in, gate_w, up_w):
    rows, columns = rows_in.shape[0], gate_w.shape[1]
    tile = 256

    def kernel(rows_ref, gate_ref, up_ref, mixed_ref, slope_ref, value_ref):
        gate_proj = fdot(rows_ref[...], gate_ref[...])
        up_proj = fdot(rows_ref[...], up_ref[...])
        gelu_value, gelu_slope = gelu_parts(gate_proj)
        mixed_ref[...] = (gelu_value * up_proj).astype(jnp.bfloat16)
        slope_ref[...] = (gelu_slope * up_proj).astype(jnp.bfloat16)
        value_ref[...] = gelu_value.astype(jnp.bfloat16)

    return pl.pallas_call(
        kernel,
        grid=(rows // tile,),
        in_specs=[row_block(tile, rows_in.shape[1]), whole_block(gate_w.shape), whole_block(up_w.shape)],
        out_specs=[row_block(tile, columns)] * 3,
        out_shape=[jax.ShapeDtypeStruct((rows, columns), jnp.bfloat16)] * 3,
    )(rows_in, gate_w, up_w)


def backward_factors(grad_rows, slope_up, value, w_down):
    rows, columns = slope_up.shape
    tile = 256

    def kernel(grad_ref, slope_ref, value_ref, down_ref, gate_ref, up_ref):
        grad_mixed = times_transposed(grad_ref[...], down_ref[...])
        gate_ref[...] = (grad_mixed * slope_ref[...].astype(jnp.float32)).astype(jnp.bfloat16)
        up_ref[...] = (grad_mixed * value_ref[...].astype(jnp.float32)).astype(jnp.bfloat16)

    return pl.pallas_call(
        kernel,
        grid=(rows // tile,),
        in_specs=[
            row_block(tile, grad_rows.shape[1]),
            row_block(tile, columns),
            row_block(tile, columns),
            whole_block(w_down.shape),
        ],
        out_specs=[row_block(tile, columns)] * 2,
        out_shape=[jax.ShapeDtypeStruct((rows, columns), jnp.bfloat16)] * 2,
    )(grad_rows, slope_up, value, w_down)


def gradient_rows(left, right, far_left, far_right, extra=None):
    rows, columns = left.shape[0], right.shape[1]
    tile = rows // 2
    operands = [left, right, far_left, far_right] + ([] if extra is None else [extra])

    def kernel(*refs):
        total = fdot(refs[0][...], refs[1][...]) + fdot(refs[2][...], refs[3][...])
        if extra is not None:
            total = total + refs[4][...].astype(jnp.float32)
        refs[-1][...] = total.astype(jnp.bfloat16)

    in_specs = [
        row_block(tile, left.shape[1]),
        whole_block(right.shape),
        row_block(tile, far_left.shape[1]),
        whole_block(far_right.shape),
        row_block(tile, columns),
    ]
    return pl.pallas_call(
        kernel,
        grid=(2,),
        in_specs=in_specs[: len(operands)],
        out_specs=row_block(tile, columns),
        out_shape=jax.ShapeDtypeStruct((rows, columns), jnp.bfloat16),
    )(*operands)


def widen_rows(received):
    peers = len(received)
    half_rows, columns = received[0].shape
    others = [swap_cores(block) for block in received]
    chunk = half_rows // 3 if half_rows % 48 == 0 else half_rows
    steps = half_rows // chunk

    def kernel(*refs):
        own = lax.axis_index("fsdp")
        core = lax.axis_index("rep") % 2
        mine = pl.program_id(0) == core
        out = refs[-1]
        for i in range(peers):
            for k in range(peers):

                @pl.when((own ^ k) == i)
                def _():
                    block = jnp.where(mine, refs[k][...], refs[peers + k][...])
                    out[:, i * columns : (i + 1) * columns] = block.astype(jnp.float32)

    return pl.pallas_call(
        kernel,
        grid=(2, steps),
        out_shape=jax.ShapeDtypeStruct((2 * half_rows, peers * columns), jnp.float32),
        in_specs=[pl.BlockSpec((chunk, columns), lambda h, i: (i, 0))] * (2 * peers),
        out_specs=pl.BlockSpec((chunk, peers * columns), lambda h, i: (h * steps + i, 0)),
    )(*received, *others)


def join_halves(mine, core):
    other = swap_cores(mine)
    first = core == 0
    return jnp.stack([jnp.where(first, mine, other), jnp.where(first, other, mine)])


def sum_to_owner(partial):
    own = lax.axis_index("fsdp")
    peers = lax.axis_size("fsdp")
    blocks = partial.reshape((peers, partial.shape[0] // peers) + partial.shape[1:])
    total = pick(blocks, own)
    for step in range(1, peers):
        sent = pick(blocks, own ^ step).astype(jnp.bfloat16)
        total = total + to_peer(sent, step).astype(jnp.float32)
    return total


def sum_over_cores(halves, core, axis=0):
    mine = pick(halves, core, axis)
    other = swap_cores(pick(halves, 1 - core, axis).astype(jnp.bfloat16))
    return (mine + other.astype(jnp.float32)).astype(jnp.bfloat16)


def add_rounded(first_op, second_op):
    return (first_op.astype(jnp.float32) + second_op.astype(jnp.float32)).astype(jnp.bfloat16)


def along_line(block, moves):
    pairs = [(2 * i + core, 2 * j + core) for i, j in moves for core in (0, 1)]
    return lax.ppermute(block, "rep", pairs)


def sum_over_pairs(block):
    pairs = lax.axis_size("rep") // 2
    if pairs != 4:
        step = 1
        while step < pairs:
            block = add_rounded(block, along_line(block, [(i, i ^ step) for i in range(pairs)]))
            step = 2 * step
        return block
    pair = lax.axis_index("rep") // 2
    inner = (pair == 1) | (pair == 2)
    block = add_rounded(block, along_line(block, [(0, 1), (3, 2)]))
    block = add_rounded(block, along_line(block, [(1, 2), (2, 1)]))
    return jnp.where(inner, block, along_line(block, [(1, 0), (2, 3)]))


def across_pairs(block):
    pairs = lax.axis_size("rep") // 2
    return [along_line(block, [(i, i ^ step) for i in range(pairs)]) for step in range(1, pairs)]


def send_across(own_rows, rows_of):
    if lax.axis_size("fsdp") != 4:
        return across_pairs(own_rows)
    return across_pairs(jnp.stack([own_rows, rows_of(lax.axis_index("fsdp") ^ 3)]))


def spread_rows(received):
    width = received[0].shape[-1]
    if lax.axis_size("fsdp") != 4:
        return gather_blocks(jnp.stack(received)).reshape(-1, width)
    own_blocks = jnp.stack([block[0] for block in received])
    near = [to_peer(own_blocks, step).reshape(-1, width) for step in (1, 2)]
    return jnp.concatenate([block.reshape(-1, width) for block in received] + near)


def rms_factor(values):
    return lax.rsqrt(jnp.mean(values * values, axis=-1, keepdims=True) + EPSILON)


def norm_back(grad_unit, unit_vals, factor):
    return factor * (
        grad_unit - unit_vals * jnp.mean(grad_unit * unit_vals, axis=-1, keepdims=True)
    )


def gelu_parts(values):
    cubic = values * values * values
    tangent = jnp.tanh(GELU_SCALE * (values + 0.044715 * cubic))
    result = 0.5 * values * (1.0 + tangent)
    slope = 0.5 * (1.0 + tangent) + 0.5 * values * (1.0 - tangent * tangent) * GELU_SCALE * (
        1.0 + 3.0 * 0.044715 * values * values
    )
    return (result, slope)


def rope_tables(positions, head_width):
    half_width = head_width // 2
    freqs = 10000.0 ** (-2.0 * jnp.arange(half_width, dtype=jnp.float32) / head_width)
    angles = positions.astype(jnp.float32)[:, None] * freqs[None, :]
    return (jnp.cos(angles), jnp.sin(angles))


def rotate(values, cos_table, sin_table):
    half_width = values.shape[-1] // 2
    lower_half = values[..., :half_width]
    upper_half = values[..., half_width:]
    return jnp.concatenate(
        [
            lower_half * cos_table - upper_half * sin_table,
            upper_half * cos_table + lower_half * sin_table,
        ],
        axis=-1,
    )


def unrotate(grads, cos_table, sin_table):
    half_width = grads.shape[-1] // 2
    lower_half = grads[..., :half_width]
    upper_half = grads[..., half_width:]
    return jnp.concatenate(
        [
            lower_half * cos_table + upper_half * sin_table,
            upper_half * cos_table - lower_half * sin_table,
        ],
        axis=-1,
    )


def locate(row_ids, lengths):
    ends = jnp.cumsum(lengths)
    starts = ends - lengths
    segment = jnp.sum((row_ids[:, None] >= ends[None, :]).astype(jnp.int32), axis=1)
    choose = segment[:, None] == jnp.arange(lengths.shape[0], dtype=jnp.int32)[None, :]
    first_row = jnp.sum(jnp.where(choose, starts[None, :], 0), axis=1)
    return (segment, row_ids - first_row)


def window_mask(query_rows, query_seg, key_rows, key_seg):
    distance = query_rows[:, None] - key_rows[None, :]
    return (
        (query_seg[:, None] == key_seg[None, :])
        & (distance >= 0)
        & (distance < WINDOW)
        & (key_rows[None, :] >= 0)
    )


def fdot(first_op, second_op):
    return jnp.dot(first_op, second_op, preferred_element_type=jnp.float32)


def times_transposed(first_op, second_op):
    return lax.dot_general(
        first_op, second_op, (((1,), (1,)), ((), ())), preferred_element_type=jnp.float32
    )


def outer_sum(first_op, second_op):
    return lax.dot_general(
        first_op, second_op, (((0,), (0,)), ((), ())), preferred_element_type=jnp.float32
    )


def body(
    block_in,
    seq_lengths,
    input_gain,
    w_query,
    w_key,
    w_value,
    query_gain,
    key_gain,
    w_out,
    post_attn_gain,
    pre_ff_gain,
    w_gate,
    w_up,
    w_down,
    post_ff_gain,
    cotangent,
):
    bf16 = jnp.bfloat16
    f32 = jnp.float32
    own = lax.axis_index("fsdp")
    peers = lax.axis_size("fsdp")
    core = lax.axis_index("rep") % 2
    rows_here, width = block_in.shape[1:]
    rows = rows_here * peers
    head_width = w_key.shape[1]
    num_heads = w_query.shape[1] // head_width
    parts = peers // num_heads
    query_count = rows // parts
    head = own // parts
    query_start = (own % parts) * query_count
    slice_rows = w_gate.shape[0]
    half_rows = slice_rows // 2
    columns = w_down.shape[0]
    out_rows = w_out.shape[0]
    gain_slice = query_gain.shape[0]

    resid_in = gather_blocks(block_in[0]).reshape(rows, width).astype(f32)

    half_of = lambda matrix: pick(matrix.reshape(2, matrix.shape[0] // 2, matrix.shape[1]), core)
    gain_parts = (input_gain, post_attn_gain, pre_ff_gain, post_ff_gain, query_gain, key_gain)
    gain_width = 3 * head_width
    gain_rows = [
        jnp.pad(part[None], ((0, 0), (0, gain_width - part.shape[0]))) for part in gain_parts
    ]
    gain_block = jnp.concatenate(gain_rows + [jnp.zeros((10, gain_width), bf16)])
    query_half = half_of(w_query)
    kv_half = jnp.concatenate([half_of(w_key), half_of(w_value)], axis=1)

    def attn_block(peer):
        mine = lax.dynamic_slice_in_dim(query_half, (peer // parts) * head_width, head_width, 1)
        return jnp.concatenate([jnp.concatenate([mine, kv_half], axis=1), gain_block])

    qkv_blocks = exchange_blocks(attn_block)
    qkv_blocks, out_half = lax.optimization_barrier((qkv_blocks, half_of(w_out)))
    qkv_all = place_halves(qkv_blocks)
    qkv_w = qkv_all[:, :, :half_rows].reshape(width, gain_width)
    gains = [
        qkv_all[:, 0, half_rows + i, : part.shape[0]].reshape(-1).astype(f32)
        for i, part in enumerate(gain_parts)
    ]
    gain_in, gain_pa, gain_pf, gain_pff, gain_q, gain_k = gains
    out_blocks = [out_half] + [to_peer(out_half, step) for step in range(1, peers)]
    out_w = place_halves(out_blocks).reshape(-1, width)

    gate_half = half_of(w_gate)
    up_half = half_of(w_up)

    def ff_block(peer):
        first = lax.dynamic_slice_in_dim(gate_half, peer * columns, columns, 1)
        second = lax.dynamic_slice_in_dim(up_half, peer * columns, columns, 1)
        return jnp.stack([first, second])

    ff_sent = [ff_block(own ^ step) for step in range(peers)]
    qkv_blocks, ff_sent = lax.optimization_barrier((qkv_blocks, ff_sent))
    ff_blocks = [ff_sent[0]] + [to_peer(ff_sent[step], step) for step in range(1, peers)]
    gate_w, up_w = [whole.reshape(width, columns) for whole in place_pairs(ff_blocks)]

    row_ids = jnp.arange(rows, dtype=jnp.int32)
    segment, positions = locate(row_ids, seq_lengths[0])
    cos_table, sin_table = rope_tables(positions, head_width)
    own_queries = lambda array: (
        array if parts == 1 else lax.dynamic_slice_in_dim(array, query_start, query_count, 0)
    )
    query_ids = own_queries(row_ids)
    query_seg = own_queries(segment)
    query_cos = own_queries(cos_table)
    query_sin = own_queries(sin_table)
    allowed = window_mask(query_ids, query_seg, row_ids, segment)
    score_scale = head_width ** (-0.5)
    unit_in = resid_in * rms_factor(resid_in)
    normed_in = (unit_in * gain_in).astype(bf16)
    qkv = fdot(normed_in, qkv_w)
    query_raw = own_queries(qkv[:, :head_width])
    key_raw = qkv[:, head_width : 2 * head_width]
    value_bf = qkv[:, 2 * head_width :].astype(bf16)
    factor_q = rms_factor(query_raw)
    unit_q = query_raw * factor_q
    factor_k = rms_factor(key_raw)
    unit_k = key_raw * factor_k
    query_rot = rotate(unit_q * gain_q, query_cos, query_sin).astype(bf16)
    key_rot = rotate(unit_k * gain_k, cos_table, sin_table).astype(bf16)
    scores = jnp.where(allowed, times_transposed(query_rot, key_rot) * score_scale, NEG_FILL)
    row_max = jnp.max(scores, axis=-1, keepdims=True)
    log_total = row_max + jnp.log(jnp.sum(jnp.exp(scores - row_max), axis=-1, keepdims=True))
    probs = jnp.exp(scores - log_total)
    probs_bf = probs.astype(bf16)
    attended_own = fdot(probs_bf, value_bf).astype(bf16)
    attended_blocks = [attended_own] + [to_peer(attended_own, step) for step in range(1, peers)]

    def store_attended(i, block, output):
        peer = peer_of(i)
        first_row = pl.multiple_of((peer % parts) * query_count, query_count)
        first_column = pl.multiple_of((peer // parts) * head_width, head_width)
        output[pl.ds(first_row, query_count), pl.ds(first_column, head_width)] = block

    attended = copy_blocks(attended_blocks, (rows, num_heads * head_width), store_attended)
    attn_proj = fdot(attended, out_w)
    factor_pa = rms_factor(attn_proj)
    unit_pa = attn_proj * factor_pa
    hidden = resid_in + unit_pa * gain_pa
    factor_hid = rms_factor(hidden)
    unit_hid = hidden * factor_hid
    normed_ff = (unit_hid * gain_pf).astype(bf16)

    own_rows = lambda array: lax.dynamic_slice_in_dim(array, own * rows_here, rows_here, 0)
    rows_of = lambda array: (
        lambda peer: lax.dynamic_slice_in_dim(array, peer * rows_here, rows_here, 0)
    )
    far_normed = send_across(own_rows(normed_ff), rows_of(normed_ff))

    mixed, slope_up, value_ff = forward_factors(normed_ff, gate_w, up_w)
    ff_proj = sum_to_owner(fdot(mixed, w_down))
    hidden_own = own_rows(hidden)
    factor_ff = rms_factor(ff_proj)
    unit_ff = ff_proj * factor_ff
    block_out = (hidden_own + unit_ff * gain_pff).astype(bf16)
    grad_out = cotangent[0].astype(f32)
    grad_gain_pff = jnp.sum(grad_out * unit_ff, axis=0)
    grad_ff_own = norm_back(grad_out * gain_pff, unit_ff, factor_ff).astype(bf16)
    grad_ff_proj = gather_blocks(grad_ff_own).reshape(rows, width)
    far_grad_ff = send_across(grad_ff_own, rows_of(grad_ff_proj))
    grad_gate, grad_up = backward_factors(grad_ff_proj, slope_up, value_ff, w_down)
    grad_normed_part = times_transposed(grad_gate, gate_w) + times_transposed(grad_up, up_w)
    grad_normed_part, far_normed = lax.optimization_barrier((grad_normed_part, far_normed))
    grad_normed_ff = sum_to_owner(grad_normed_part)
    far_normed = spread_rows(far_normed)
    factor_hid_own = own_rows(factor_hid)
    unit_hid_own = hidden_own * factor_hid_own
    grad_gain_pf = jnp.sum(grad_normed_ff * unit_hid_own, axis=0)
    grad_hidden = grad_out + norm_back(grad_normed_ff * gain_pf, unit_hid_own, factor_hid_own)
    factor_pa_own = own_rows(factor_pa)
    unit_pa_own = own_rows(attn_proj) * factor_pa_own
    grad_gain_pa = jnp.sum(grad_hidden * unit_pa_own, axis=0)
    grad_attn_own = norm_back(grad_hidden * gain_pa, unit_pa_own, factor_pa_own).astype(bf16)
    grad_attn_proj = gather_blocks(grad_attn_own).reshape(rows, width)

    far_mixed, far_slope_up, far_value = forward_factors(far_normed, gate_w, up_w)
    grad_attn_proj, far_slope_up, far_grad_ff = lax.optimization_barrier(
        (grad_attn_proj, far_slope_up, far_grad_ff)
    )
    far_grad_ff = spread_rows(far_grad_ff)
    far_grad_gate, far_grad_up = backward_factors(far_grad_ff, far_slope_up, far_value, w_down)
    split_columns = lambda array: array.T.reshape(peers, 2, half_rows, array.shape[0])
    rows_for = lambda split, half: pick(split, half, 1).reshape(peers * half_rows, -1)
    normed_split = split_columns(normed_ff)
    far_split = split_columns(far_normed)

    def split_rows(own_part, far_part):
        half_for = lambda half, extra: gradient_rows(
            rows_for(normed_split, half), own_part, rows_for(far_split, half), far_part, extra
        )
        other = swap_cores(half_for(1 - core, None))
        part = half_for(core, other).reshape(peers, half_rows, columns)
        return widen_rows(exchange_blocks(lambda peer: pick(part, peer)))

    share_gate = split_rows(grad_gate, far_grad_gate)
    share_up = split_rows(grad_up, far_grad_up)
    down_grad = outer_sum(mixed, grad_ff_proj) + outer_sum(far_mixed, far_grad_ff)
    down_grad = down_grad.astype(bf16)
    share_down = down_grad.astype(f32) + swap_cores(down_grad).astype(f32)

    out_head = lax.dynamic_slice_in_dim(out_w, head * head_width, head_width, 0)
    attended_cols = lax.dynamic_slice_in_dim(attended, own * out_rows, out_rows, 1)
    if parts == 1:
        out_head = w_out
        attended_cols = attended_own
    out_grad = outer_sum(attended_cols, grad_attn_proj)
    grad_attended = times_transposed(own_queries(grad_attn_proj), out_head).astype(bf16)
    grad_probs = times_transposed(grad_attended, value_bf)
    delta = jnp.sum(
        grad_attended.astype(f32) * attended_own.astype(f32), axis=-1, keepdims=True
    )
    grad_scores = (probs * (grad_probs - delta) * score_scale).astype(bf16)
    grad_value = outer_sum(probs_bf, grad_attended).astype(bf16)
    grad_key_rot = outer_sum(grad_scores, query_rot)
    grad_query_rot = fdot(grad_scores, key_rot)
    grad_unit_q = unrotate(grad_query_rot, query_cos, query_sin)
    grad_unit_k = unrotate(grad_key_rot, cos_table, sin_table)
    grad_gain_q = jnp.sum(grad_unit_q * unit_q, axis=0)
    grad_gain_k = jnp.sum(grad_unit_k * unit_k, axis=0)
    grad_query = norm_back(grad_unit_q * gain_q, unit_q, factor_q).astype(bf16)
    grad_key = norm_back(grad_unit_k * gain_k, unit_k, factor_k).astype(bf16)
    if parts > 1:
        grad_query = lax.dynamic_update_slice_in_dim(
            jnp.zeros((rows, head_width), bf16), grad_query, query_start, 0
        )
    grad_qkv = jnp.concatenate([grad_query, grad_key, grad_value], axis=1)
    grad_normed_in = sum_to_owner(times_transposed(grad_qkv, qkv_w))
    qkv_grad = outer_sum(normed_in, grad_qkv)
    resid_own = block_in[0].astype(f32)
    factor_in_own = rms_factor(resid_own)
    unit_in_own = resid_own * factor_in_own
    grad_gain_in = jnp.sum(grad_normed_in * unit_in_own, axis=0)
    grad_input = (
        grad_hidden + norm_back(grad_normed_in * gain_in, unit_in_own, factor_in_own)
    ).astype(bf16)

    gain_grads = (
        grad_gain_in,
        grad_gain_pa,
        grad_gain_pf,
        grad_gain_pff,
        grad_gain_q,
        grad_gain_k,
    )
    gain_sums = jnp.concatenate([part.reshape(peers, -1) for part in gain_grads], axis=1)
    gain_count = gain_sums.shape[1] // 2
    gain_sums = jnp.pad(
        gain_sums.reshape(peers, 2, 1, gain_count),
        ((0, 0), (0, 0), (0, 15), (0, 3 * head_width - gain_count)),
    )
    attn_grads = jnp.concatenate(
        [qkv_grad.reshape(peers, 2, half_rows, 3 * head_width), gain_sums], axis=2
    )
    attn_half = sum_over_cores(attn_grads, core, 1)
    received = exchange_blocks(lambda peer: pick(attn_half, peer))
    received = in_order(received).astype(f32)
    heads_sum = received[:, :half_rows, :head_width].reshape(
        num_heads, parts, half_rows, head_width
    )
    heads_sum = jnp.sum(heads_sum, axis=1)
    query_part = jnp.concatenate([heads_sum[i] for i in range(num_heads)], axis=1)
    rest = jnp.sum(received, axis=0)
    kv_part = rest[:half_rows, head_width:]
    out_half = sum_over_cores(out_grad.reshape(2, out_rows // 2, width), core)
    qkv_half = jnp.concatenate([query_part, kv_part], axis=1).astype(bf16)
    gain_half = rest[half_rows:].astype(bf16)
    qkv_rows = qkv_half.size // width
    half_out = out_rows // 2
    gain_pad = jnp.pad(gain_half[0], (0, 16 * width - gain_half.shape[1])).reshape(16, width)
    small = sum_over_pairs(
        jnp.concatenate([qkv_half.reshape(qkv_rows, width), out_half, gain_pad], axis=0)
    )
    small = join_halves(small, core).astype(f32)
    share_qkv = small[:, :qkv_rows].reshape(slice_rows, (num_heads + 2) * head_width)
    query_width = num_heads * head_width
    share_query = share_qkv[:, :query_width]
    share_key = share_qkv[:, query_width : query_width + head_width]
    share_value = share_qkv[:, query_width + head_width :]
    share_out = small[:, qkv_rows : qkv_rows + half_out].reshape(out_rows, width)
    gain_line = small[:, qkv_rows + half_out, :gain_count].reshape(-1)
    sections = [slice_rows, slice_rows, slice_rows, slice_rows, gain_slice, gain_slice]
    shares = []
    start = 0
    for size in sections:
        shares.append(gain_line[start : start + size])
        start = start + size
    share_in, share_pa, share_pf, share_pff, share_q, share_k = shares
    return (
        block_out[None],
        grad_input[None],
        share_in,
        share_query,
        share_key,
        share_value,
        share_q,
        share_k,
        share_out,
        share_pa,
        share_pf,
        share_gate,
        share_up,
        share_down,
        share_pff,
    )


def solution(mesh):
    placed = (
        P("rep", "fsdp", None),
        P("rep", None),
        P("fsdp"),
        P("fsdp", None),
        P("fsdp", None),
        P("fsdp", None),
        P("fsdp"),
        P("fsdp"),
        P("fsdp", None),
        P("fsdp"),
        P("fsdp"),
        P("fsdp", None),
        P("fsdp", None),
        P("fsdp", None),
        P("fsdp"),
        P("rep", "fsdp", None),
    )
    return jax.shard_map(
        body,
        mesh=mesh,
        in_specs=placed,
        out_specs=(
            P("rep", "fsdp", None),
            P("rep", "fsdp", None),
            P("fsdp"),
            P("fsdp", None),
            P("fsdp", None),
            P("fsdp", None),
            P("fsdp"),
            P("fsdp"),
            P("fsdp", None),
            P("fsdp"),
            P("fsdp"),
            P("fsdp", None),
            P("fsdp", None),
            P("fsdp", None),
            P("fsdp"),
        ),
        check_vma=False,
    )
```
